32 devices in a mesh: groups: 2 (over y), space: 4 (over z), tm: 4 (over x, core).
Axes of the slice: x: 2, y: 2, z: 4, core: 2. Of those that a mesh axis runs over, the one named last changes fastest.
Arguments:
- state: float32 [8, 4, 256, 256], P(('groups', 'tm'), 'space'), parts along dimension 0, may hold values from 0 to 1
- classes: int32 [8, 256, 256], P(('groups', 'space')), parts along dimension 0, may hold values from 0 to 3
- perm_table: float32 [4], replicated, may hold values from 0.2 to 2
- rate_table: float32 [4], replicated, may hold values from 0.02 to 1
Outputs:
- new_state: float32 [8, 4, 256, 256], P(('groups', 'tm'), 'space'), parts along dimension 0
The draws below stay inside these ranges and needn't reach their ends.
There are 2 independent parts, one for each index of `groups`. The reference program is written for one: setup_inputs(seed, part) draws one part's arguments, and reference() takes and returns one part's arrays. A program takes and returns all parts, laid end to end along the dimension named above; an argument that names none is the same for every part. Nothing has to cross between parts.
All inputs are finite; a program needn't handle non-finite values.
Results may differ from the reference program's by a relative error of at most 0.0001.
Values sent between devices are 32-bit elements; how exact they have to be, the bound alone decides.
No kernel may reach another device: no remote copies, remote signals or barrier semaphores. Data moves between devices by JAX's collectives and lax.ppermute only.
A program may use at most 64 MiB of HBM per device.

```python
import math
import jax
import jax.numpy as jnp

NY = 256
NZ = 256
ITERS = 3
FINE = 2
CLASSES = 4
NT = 4
NX = 4


def set_ends(values, stream_key, smallest, top_value):
    shape = values.shape
    index_at = [jax.random.randint(jax.random.fold_in(stream_key, axis), (), 0, shape[axis]) for axis in range(len(shape))]
    values = values.at[tuple(index_at)].set(smallest)
    longest = shape.index(max(shape))
    index_at[longest] = (index_at[longest] + 1) % shape[longest]
    return values.at[tuple(index_at)].set(top_value)


def levels(rng, shape, cuts, low, high):
    loudness = 1.0
    for position, shards_of in cuts:
        steps = jax.random.uniform(jax.random.fold_in(jax.random.fold_in(rng, 6), position), (shards_of,), jnp.float32, low / len(cuts), high / len(cuts))
        loudness = loudness * jnp.repeat(jnp.exp(steps), shape[position] // shards_of).reshape((-1,) + (1,) * (len(shape) - 1 - position))
    return loudness


def setup_inputs(seed: int = 0, part: int = 0) -> dict:
    streams_of = jax.random.split(jax.random.key(seed), 5)
    own_keys = jax.random.split(jax.random.fold_in(streams_of[4], part), 5)
    state = jnp.clip(1.0 * jax.random.uniform(own_keys[0], (NT, NX, NY, NZ), jnp.float32) ** levels(own_keys[0], (NT, NX, NY, NZ), ((0, 4), (1, 4)), -0.2, 0.2), 0.0, 1.0)
    classes = set_ends(jax.random.randint(own_keys[1], (NX, NY, NZ), 0, CLASSES), jax.random.fold_in(own_keys[1], 1), 0, CLASSES - 1).astype(jnp.int32)
    perm_table = jnp.clip(jnp.exp(jax.random.uniform(streams_of[2], (CLASSES,), jnp.float32, math.log(0.2), math.log(2.0))), 0.2, 2.0)
    rate_table = jnp.clip(jnp.exp(jax.random.uniform(streams_of[3], (CLASSES,), jnp.float32, math.log(0.02), math.log(1.0))), 0.02, 1.0)
    return dict(state=state, classes=classes, perm_table=perm_table, rate_table=rate_table)


DIFF = 2.0
ADV = 0.25


def restrict(field):
    cx, ny, nz = field.shape
    return field.reshape(cx, ny // 2, 2, nz // 2, 2).mean(axis=(2, 4))


def prolong(coarse):
    return jnp.repeat(jnp.repeat(coarse, 2, axis=1), 2, axis=2)


def vertical(field):
    zero_plane = jnp.zeros(field.shape[:2] + (1,), jnp.float32)
    upper = jnp.concatenate([field[:, :, 1:], zero_plane], axis=2)
    lower = jnp.concatenate([zero_plane, field[:, :, :-1]], axis=2)
    return upper, lower


def operate(field):
    upper, lower = vertical(field)
    beside = jnp.roll(field, -1, 0) + jnp.roll(field, 1, 0)
    beside = beside + jnp.roll(field, -1, 1) + jnp.roll(field, 1, 1)
    beside = beside + upper + lower
    return (1.0 + 6.0 * DIFF) * field - DIFF * beside


def fine_step(field, perm):
    upper, lower = vertical(field)
    rhs = field - ADV * perm * field * (upper - lower)
    solution = field
    residual = rhs - operate(solution)
    direction = residual
    norm_now = jnp.sum(residual * residual)
    for step in range(ITERS):
        image = operate(direction)
        alpha = norm_now / jnp.sum(direction * image)
        solution = solution + alpha * direction
        residual = residual - alpha * image
        norm_next = jnp.sum(residual * residual)
        direction = residual + (norm_next / norm_now) * direction
        norm_now = norm_next
    return solution


def reference(state, classes, perm_table, rate_table):
    perm = perm_table[classes]
    rate = rate_table[classes]
    coarse_ratio = 1.0 / (1.0 + restrict(rate))
    jumps = []
    for slice_index in range(NT):
        field = state[slice_index]
        for step in range(FINE):
            field = fine_step(field, perm)
        jumps.append(field - prolong(coarse_ratio * restrict(state[slice_index])))
    outputs = [state[0]]
    coarse = restrict(state[0])
    for slice_index in range(1, NT):
        jump = jumps[slice_index - 1]
        outputs.append(prolong(coarse_ratio * coarse) + jump)
        coarse = coarse_ratio * coarse + restrict(jump)
    return jnp.stack(outputs, axis=0)
```

```python
import jax
import jax.numpy as jnp
from jax import lax
from jax.experimental import pallas as pl
from jax.experimental.pallas import tpu as pltpu
from jax.sharding import PartitionSpec as P

ITERS = 3
FINE = 2


DIFF = 2.0
ADV = 0.25

PAD = 8
ROWS = 16
MOST_PLANES = 8


def with_halo(array, sides, width):
    for axis, dim in sides:
        devices, length = (lax.axis_size(axis), array.shape[dim])
        up = [(i, (i + 1) % devices) for i in range(devices)]
        down = [(j, i) for i, j in up]
        last = lax.slice_in_dim(array, length - width, length, axis=dim)
        first = lax.slice_in_dim(array, 0, width, axis=dim)
        before = lax.ppermute(last, axis, up)
        after = lax.ppermute(first, axis, down)
        array = jnp.concatenate([before, array, after], axis=dim)
    return array


def passed_along(array, axis, by):
    devices = lax.axis_size(axis)
    pairs = [(i, i + by) for i in range(devices) if 0 <= i + by < devices]
    return lax.ppermute(array, axis, pairs)


def lookup(table, classes):
    values = jnp.zeros(classes.shape, jnp.float32)
    for entry in range(table.shape[0]):
        values = jnp.where(classes == entry, table[entry], values)
    return values


def restrict(field):
    cx, ny, nz = field.shape
    return field.reshape(cx, ny // 2, 2, nz // 2, 2).mean(axis=(2, 4))


def prolong(coarse):
    return jnp.repeat(jnp.repeat(coarse, 2, axis=1), 2, axis=2)


def vertical(field):
    zero_plane = jnp.zeros(field.shape[:2] + (1,), jnp.float32)
    upper = jnp.concatenate([field[:, :, 1:], zero_plane], axis=2)
    lower = jnp.concatenate([zero_plane, field[:, :, :-1]], axis=2)
    return (upper, lower)


def operate(field):
    padded = with_halo(field, (("space", 0),), 1)
    upper, lower = vertical(field)
    beside = padded[2:] + padded[:-2]
    beside = beside + jnp.roll(field, -1, 1) + jnp.roll(field, 1, 1)
    beside = beside + upper + lower
    return (1.0 + 6.0 * DIFF) * field - DIFF * beside


def squares(residual):
    return lax.psum(jnp.sum(residual * residual), "space")


def fine_step(field, perm):
    upper, lower = vertical(field)
    rhs = field - ADV * perm * field * (upper - lower)
    solution = field
    residual = rhs - operate(solution)
    direction = residual
    norm_now = squares(residual)
    for step in range(ITERS):
        image = operate(direction)
        alpha = norm_now / lax.psum(jnp.sum(direction * image), "space")
        solution = solution + alpha * direction
        residual = residual - alpha * image
        norm_next = squares(residual)
        direction = residual + norm_next / norm_now * direction
        norm_now = norm_next
    return solution


def spread_body(state, classes, perm_table, rate_table):
    start = state[0]
    perm = lookup(perm_table, classes)
    coarse_ratio = 1.0 / (1.0 + restrict(lookup(rate_table, classes)))
    field = start
    for step in range(FINE):
        field = fine_step(field, perm)
    coarse_start = restrict(start)
    jump = field - prolong(coarse_ratio * coarse_start)
    jump_coarse = restrict(jump)
    first = lax.axis_index("tm") == 0
    factor = jnp.where(first, 0.0, coarse_ratio)
    offset = jnp.where(first, coarse_ratio * coarse_start + jump_coarse, jump_coarse)
    before = passed_along(jump, "tm", 1)
    before_coarse = restrict(before)

    def relay_turn(turn, carry):
        outgoing, received = carry
        received = passed_along(outgoing, "tm", 1)
        return (factor * received + offset, received)

    outgoing, received = lax.fori_loop(
        0, lax.axis_size("tm") - 1, relay_turn, (offset, jnp.zeros_like(offset))
    )
    updated = jnp.where(first, start, before + prolong(received - before_coarse))
    return updated[None]


def beside_in_plane(block, lane, cells):
    rows = block.shape[0]
    inner = block[PAD:rows - PAD]
    after = pltpu.roll(block, rows - 1, 0)[PAD:rows - PAD]
    before = pltpu.roll(block, 1, 0)[PAD:rows - PAD]
    upper = jnp.where(lane == cells - 1, 0.0, pltpu.roll(inner, cells - 1, 1))
    lower = jnp.where(lane == 0, 0.0, pltpu.roll(inner, 1, 1))
    return inner, after + before, upper, lower


def gram_steps(g00, g01, g11, g12, g22, h22):
    a = 1.0 + 6.0 * DIFF
    b = 6.0 * DIFF
    g02 = 2.0 * g11 - g00
    h00, h01, h02 = g01, g11, g12
    h11, h12 = 0.5 * (g12 + g01), 0.5 * (g22 + g02)
    rr = g00
    alpha0 = rr / (a * g00 - b * h00)
    p, q = 1.0 - a * alpha0, b * alpha0
    new = p * p * g00 + 2.0 * p * q * g01 + q * q * g11
    beta = new / rr
    rr = new
    e, f = p + beta, q
    dd = e * e * g00 + 2.0 * e * f * g01 + f * f * g11
    dmd = e * e * h00 + 2.0 * e * f * h01 + f * f * h11
    alpha1 = rr / (a * dd - b * dmd)
    u = p - alpha1 * (a * e - 0.5 * b * f)
    v = q - alpha1 * (a * f - b * e)
    w = alpha1 * (0.5 * b) * f
    new = (u * u * g00 + v * v * g11 + w * w * g22
           + 2.0 * (u * v * g01 + u * w * g02 + v * w * g12))
    beta = new / rr
    rr = new
    u, v = u + beta * e, v + beta * f
    dd = (u * u * g00 + v * v * g11 + w * w * g22
          + 2.0 * (u * v * g01 + u * w * g02 + v * w * g12))
    dmd = (u * u * h00 + v * v * h11 + w * w * h22
           + 2.0 * (u * v * h01 + u * w * h02 + v * w * h12))
    alpha2 = rr / (a * dd - b * dmd)
    return (alpha0 + alpha1 * e + alpha2 * u, alpha1 * f + alpha2 * v, alpha2 * w)


def fine_kernel(planes, ny, nz, table_len):
    chunks = ny // ROWS

    def kernel(table, *refs):
        state_in = refs[:planes]
        classes_in = refs[planes:2 * planes]
        outs = refs[2 * planes:3 * planes]
        x, r, p1, p2, perm, sems = refs[3 * planes:]
        copies = []
        for i in range(planes):
            src = state_in[i]
            parts = (
                (src, x.at[i, pl.ds(PAD, ny)]),
                (src.at[pl.ds(ny - PAD, PAD)], x.at[i, pl.ds(0, PAD)]),
                (src.at[pl.ds(0, PAD)], x.at[i, pl.ds(PAD + ny, PAD)]),
                (classes_in[i], perm.at[i]),
            )
            for k, (a, b) in enumerate(parts):
                copies.append(pltpu.make_async_copy(a, b, sems.at[i, k]))
        for copy in copies:
            copy.start()
        for copy in copies:
            copy.wait()
        lane = lax.broadcasted_iota(jnp.int32, (ROWS, nz), 1)
        zero = jnp.zeros((8, nz), jnp.float32)

        def folded(value):
            total = value[:8]
            for k in range(8, ROWS, 8):
                total = total + value[k:k + 8]
            return total

        def total(acc):
            return jnp.sum(jnp.sum(acc, axis=1, keepdims=True), axis=0, keepdims=True)

        def wrap(field):
            for i in range(planes):
                field[i, pl.ds(0, PAD)] = field[i, pl.ds(ny, PAD)]
                field[i, pl.ds(PAD + ny, PAD)] = field[i, pl.ds(PAD, PAD)]

        def stencil(field, row):
            parts = []
            for i in range(planes):
                block = field[i, pl.ds(row, ROWS + 2 * PAD)]
                parts.append(beside_in_plane(block, lane, nz))
            result = []
            for i in range(planes):
                inner, along_y, upper, lower = parts[i]
                along_x = parts[i - 1][0] + parts[(i + 1) % planes][0]
                result.append((inner, along_x + along_y + (upper + lower), upper, lower))
            return result

        for step in range(FINE):
            last = step == FINE - 1

            def first_pass(c, g00):
                row = pl.multiple_of(c * ROWS, ROWS)
                for i, (v, six, upper, lower) in enumerate(stencil(x, row)):
                    kind = perm[i, pl.ds(row, ROWS)]
                    k = jnp.zeros((ROWS, nz), jnp.float32)
                    for entry in range(table_len):
                        k = jnp.where(kind == entry, table[entry], k)
                    value = DIFF * six - (6.0 * DIFF) * v - ADV * k * v * (upper - lower)
                    r[i, pl.ds(row + PAD, ROWS)] = value
                    g00 = g00 + folded(value * value)
                return g00

            g00 = lax.fori_loop(0, chunks, first_pass, zero)
            wrap(r)

            def second_pass(c, carry):
                g01, g11 = carry
                row = pl.multiple_of(c * ROWS, ROWS)
                for i, (v, six, _, _) in enumerate(stencil(r, row)):
                    value = six * (1.0 / 6.0)
                    p1[i, pl.ds(row + PAD, ROWS)] = value
                    g01 = g01 + folded(value * v)
                    g11 = g11 + folded(value * value)
                return g01, g11

            g01, g11 = lax.fori_loop(0, chunks, second_pass, (zero, zero))
            wrap(p1)

            def third_pass(c, carry):
                g12, g22 = carry
                row = pl.multiple_of(c * ROWS, ROWS)
                for i, (v, six, _, _) in enumerate(stencil(p1, row)):
                    value = six * (1.0 / 3.0) - r[i, pl.ds(row + PAD, ROWS)]
                    p2[i, pl.ds(row + PAD, ROWS)] = value
                    g12 = g12 + folded(value * v)
                    g22 = g22 + folded(value * value)
                return g12, g22

            g12, g22 = lax.fori_loop(0, chunks, third_pass, (zero, zero))
            wrap(p2)

            def fourth_pass(c, h22):
                row = pl.multiple_of(c * ROWS, ROWS)
                inner = []
                for i in range(planes):
                    block = p2[i, pl.ds(row, ROWS + 2 * PAD)]
                    rows = ROWS + 2 * PAD
                    v = block[PAD:rows - PAD]
                    after = pltpu.roll(block, rows - 1, 0)[PAD:rows - PAD]
                    upper = jnp.where(lane == nz - 1, 0.0, pltpu.roll(v, nz - 1, 1))
                    inner.append((v, after + upper))
                for i in range(planes):
                    v, some = inner[i]
                    h22 = h22 + folded(v * (some + inner[(i + 1) % planes][0]))
                return h22

            h22 = lax.fori_loop(0, chunks, fourth_pass, zero)
            c0, c1, c2 = gram_steps(
                total(g00), total(g01), total(g11), total(g12), total(g22),
                total(h22) * (1.0 / 3.0))

            def last_pass(c, carry):
                row = pl.multiple_of(c * ROWS, ROWS)
                rows = pl.ds(row + PAD, ROWS)
                for i in range(planes):
                    value = (x[i, rows] + c0 * r[i, rows]) + (c1 * p1[i, rows] + c2 * p2[i, rows])
                    if last:
                        outs[i][pl.ds(row, ROWS)] = value
                    else:
                        x[i, rows] = value
                return carry

            lax.fori_loop(0, chunks, last_pass, 0)
            if not last:
                wrap(x)

    return kernel


def fine_steps(state_planes, classes_planes, table):
    planes = len(state_planes)
    ny, nz = state_planes[0].shape
    any_space = pl.BlockSpec(memory_space=pl.ANY)
    field = pltpu.VMEM((planes, ny + 2 * PAD, nz), jnp.float32)
    return pl.pallas_call(
        fine_kernel(planes, ny, nz, table.shape[0]),
        out_shape=[jax.ShapeDtypeStruct((ny, nz), jnp.float32)] * planes,
        in_specs=[pl.BlockSpec(memory_space=pltpu.SMEM)] + [any_space] * (2 * planes),
        out_specs=[pl.BlockSpec(memory_space=pltpu.VMEM)] * planes,
        scratch_shapes=[field, field, field, field,
                        pltpu.VMEM((planes, ny, nz), jnp.int32),
                        pltpu.SemaphoreType.DMA((planes, 4))],
        compiler_params=pltpu.CompilerParams(vmem_limit_bytes=48 * 1024 * 1024),
        name="fine_steps",
    )(table, *state_planes, *classes_planes)


def pairs_matrix(coarse, fine, transposed):
    shape = (fine, coarse) if transposed else (coarse, fine)
    along_coarse = lax.broadcasted_iota(jnp.int32, shape, 1 if transposed else 0)
    along_fine = lax.broadcasted_iota(jnp.int32, shape, 0 if transposed else 1)
    return jnp.where(along_fine // 2 == along_coarse, 1.0, 0.0).astype(jnp.float32)


def exact_dot(a, b):
    return jnp.dot(a, b, precision=lax.Precision.HIGHEST, preferred_element_type=jnp.float32)


def restrict_plane(field):
    ny, nz = field.shape
    rows = exact_dot(pairs_matrix(ny // 2, ny, False), field)
    return 0.25 * exact_dot(rows, pairs_matrix(nz // 2, nz, True))


def prolong_plane(coarse):
    cy, cz = coarse.shape
    rows = exact_dot(pairs_matrix(cy, 2 * cy, True), coarse)
    return exact_dot(rows, pairs_matrix(cz, 2 * cz, False))


def ratio_plane(classes, rate_table):
    ny, nz = classes.shape

    def kernel(table, kind, out):
        rate = jnp.zeros((ny, nz), jnp.float32)
        for entry in range(rate_table.shape[0]):
            rate = jnp.where(kind[...] == entry, table[entry], rate)
        out[...] = 1.0 / (1.0 + restrict_plane(rate))

    return pl.pallas_call(
        kernel,
        out_shape=jax.ShapeDtypeStruct((ny // 2, nz // 2), jnp.float32),
        in_specs=[pl.BlockSpec(memory_space=pltpu.SMEM), pl.BlockSpec(memory_space=pltpu.VMEM)],
        out_specs=pl.BlockSpec(memory_space=pltpu.VMEM),
        name="ratio",
    )(rate_table, classes)


def settle(which, candidates, start):
    ny, nz = start.shape
    count = len(candidates)

    def kernel(choice, *refs):
        own, end, diff, sem = refs[count], refs[count + 1], refs[count + 2], refs[count + 3]
        for k in range(count):
            @pl.when(choice[0] == k)
            def _():
                copy = pltpu.make_async_copy(refs[k], end, sem)
                copy.start()
                copy.wait()
        diff[...] = restrict_plane(end[...] - own[...])

    return pl.pallas_call(
        kernel,
        out_shape=[jax.ShapeDtypeStruct((ny, nz), jnp.float32),
                   jax.ShapeDtypeStruct((ny // 2, nz // 2), jnp.float32)],
        in_specs=[pl.BlockSpec(memory_space=pltpu.SMEM)]
        + [pl.BlockSpec(memory_space=pl.ANY)] * count
        + [pl.BlockSpec(memory_space=pltpu.VMEM)],
        out_specs=[pl.BlockSpec(memory_space=pltpu.VMEM)] * 2,
        scratch_shapes=[pltpu.SemaphoreType.DMA(())],
        name="settle",
    )(which, *candidates, start)


def correct(first, ratio, diffs, end, start):
    ny, nz = start.shape
    count = len(diffs)

    def kernel(is_first, share, *refs):
        end_ref, start_ref, out = refs[count:]
        drift = jnp.zeros((ny // 2, nz // 2), jnp.float32)
        for k in reversed(range(count)):
            drift = share[...] * (drift + refs[k][...])
        moved = end_ref[...] + prolong_plane(drift)
        out[...] = jnp.where(is_first[0] == 1, start_ref[...], moved)

    vmem = pl.BlockSpec(memory_space=pltpu.VMEM)
    return pl.pallas_call(
        kernel,
        out_shape=jax.ShapeDtypeStruct((ny, nz), jnp.float32),
        in_specs=[pl.BlockSpec(memory_space=pltpu.SMEM)] + [vmem] * (count + 3),
        out_specs=vmem,
        name="correct",
    )(first, ratio, *diffs, end, start)


def gathered_body(state, classes, perm_table, rate_table):
    start = state[0, 0]
    kinds = classes[0]
    width, slices = lax.axis_size("space"), lax.axis_size("tm")
    axes = ("space", "tm")
    place = lambda s, t: (s % width) * slices + t
    site = lambda j: (width // 2 - 1 + j % 2) % width
    used = range(slices - 1)
    state_planes = [
        lax.ppermute(start, axes, [(place(site(j) + k, j), place(site(j), j + 1)) for j in used])
        for k in range(width)
    ]
    classes_planes = [kinds] + [
        lax.ppermute(kinds, axes, [(place(site(j) + k, j + 1), place(site(j), j + 1)) for j in used])
        for k in range(1, width)
    ]
    ratio = ratio_plane(kinds, rate_table)
    ends = fine_steps(state_planes, classes_planes, perm_table)
    candidates = [ends[0]] + [
        lax.ppermute(ends[k], axes, [(place(site(j), j + 1), place(site(j) + k, j + 1)) for j in used])
        for k in range(1, width)
    ]
    turn = lax.axis_index("tm")
    which = (lax.axis_index("space") - site(turn - 1)) % width
    end, diff = settle(which.astype(jnp.int32)[None], candidates, start)
    diffs = [
        lax.ppermute(diff, "tm", [(i, i + k) for i in range(1, slices - k)])
        for k in range(1, slices - 1)
    ]
    new = correct((turn == 0).astype(jnp.int32)[None], ratio, diffs, end, start)
    return new[None, None]


def body(state, classes, perm_table, rate_table):
    width = lax.axis_size("space")
    one_plane = state.shape[:2] == (1, 1) and classes.shape[0] == 1
    if one_plane and 2 < width <= MOST_PLANES and lax.axis_size("tm") > 2:
        return gathered_body(state, classes, perm_table, rate_table)
    return spread_body(state, classes, perm_table, rate_table)


def solution(mesh):
    placed = (
        P(("groups", "tm"), "space", None, None),
        P(("groups", "space"), None, None),
        P(),
        P(),
    )
    return jax.shard_map(
        body,
        mesh=mesh,
        in_specs=placed,
        out_specs=P(("groups", "tm"), "space", None, None),
        check_vma=False,
    )
```

```python
import jax
import jax.numpy as jnp
from jax import lax
from jax.experimental import pallas as pl
from jax.experimental.pallas import tpu as pltpu
from jax.sharding import PartitionSpec as P

ITERS = 3
FINE = 2


DIFF = 2.0
ADV = 0.25

SUB = 8
LANES = 128
DEPTH = 2
MOST_PLANES = 8
VMEM_BYTES = 16 * 1024 * 1024


def with_halo(array, sides, width):
    for axis, dim in sides:
        devices, length = (lax.axis_size(axis), array.shape[dim])
        up = [(i, (i + 1) % devices) for i in range(devices)]
        down = [(j, i) for i, j in up]
        last = lax.slice_in_dim(array, length - width, length, axis=dim)
        first = lax.slice_in_dim(array, 0, width, axis=dim)
        before = lax.ppermute(last, axis, up)
        after = lax.ppermute(first, axis, down)
        array = jnp.concatenate([before, array, after], axis=dim)
    return array


def passed_along(array, axis, by):
    devices = lax.axis_size(axis)
    pairs = [(i, i + by) for i in range(devices) if 0 <= i + by < devices]
    return lax.ppermute(array, axis, pairs)


def lookup(table, classes):
    values = jnp.zeros(classes.shape, jnp.float32)
    for entry in range(table.shape[0]):
        values = jnp.where(classes == entry, table[entry], values)
    return values


def restrict(field):
    cx, ny, nz = field.shape
    return field.reshape(cx, ny // 2, 2, nz // 2, 2).mean(axis=(2, 4))


def prolong(coarse):
    return jnp.repeat(jnp.repeat(coarse, 2, axis=1), 2, axis=2)


def vertical(field):
    zero_plane = jnp.zeros(field.shape[:2] + (1,), jnp.float32)
    upper = jnp.concatenate([field[:, :, 1:], zero_plane], axis=2)
    lower = jnp.concatenate([zero_plane, field[:, :, :-1]], axis=2)
    return (upper, lower)


def operate(field):
    padded = with_halo(field, (("space", 0),), 1)
    upper, lower = vertical(field)
    beside = padded[2:] + padded[:-2]
    beside = beside + jnp.roll(field, -1, 1) + jnp.roll(field, 1, 1)
    beside = beside + upper + lower
    return (1.0 + 6.0 * DIFF) * field - DIFF * beside


def squares(residual):
    return lax.psum(jnp.sum(residual * residual), "space")


def fine_step(field, perm):
    upper, lower = vertical(field)
    rhs = field - ADV * perm * field * (upper - lower)
    solution = field
    residual = rhs - operate(solution)
    direction = residual
    norm_now = squares(residual)
    for step in range(ITERS):
        image = operate(direction)
        alpha = norm_now / lax.psum(jnp.sum(direction * image), "space")
        solution = solution + alpha * direction
        residual = residual - alpha * image
        norm_next = squares(residual)
        direction = residual + norm_next / norm_now * direction
        norm_now = norm_next
    return solution


def spread_body(state, classes, perm_table, rate_table):
    start = state[0]
    perm = lookup(perm_table, classes)
    coarse_ratio = 1.0 / (1.0 + restrict(lookup(rate_table, classes)))
    field = start
    for step in range(FINE):
        field = fine_step(field, perm)
    coarse_start = restrict(start)
    jump = field - prolong(coarse_ratio * coarse_start)
    jump_coarse = restrict(jump)
    first = lax.axis_index("tm") == 0
    factor = jnp.where(first, 0.0, coarse_ratio)
    offset = jnp.where(first, coarse_ratio * coarse_start + jump_coarse, jump_coarse)
    before = passed_along(jump, "tm", 1)
    before_coarse = restrict(before)

    def relay_turn(turn, carry):
        outgoing, received = carry
        received = passed_along(outgoing, "tm", 1)
        return (factor * received + offset, received)

    outgoing, received = lax.fori_loop(
        0, lax.axis_size("tm") - 1, relay_turn, (offset, jnp.zeros_like(offset))
    )
    updated = jnp.where(first, start, before + prolong(received - before_coarse))
    return updated[None]


def in_vmem(count):
    return [pl.BlockSpec(memory_space=pltpu.VMEM)] * count


def anywhere(count):
    return [pl.BlockSpec(memory_space=pl.ANY)] * count


def in_smem(count):
    return [pl.BlockSpec(memory_space=pltpu.SMEM)] * count


def small_vmem():
    return pltpu.CompilerParams(vmem_limit_bytes=VMEM_BYTES)


def strips_shape(ny, nz, extra=0):
    return (nz // LANES, ny // SUB + extra, SUB, LANES)


def halves_of(plane, halves, sems):
    return [
        pltpu.make_async_copy(plane.at[:, pl.ds(h * LANES, LANES)], halves.at[h], sems.at[h])
        for h in range(halves.shape[0])
    ]


def strip(halves, h, o, strips):
    return halves[h, pl.ds(o, SUB, stride=strips)]


def pairs(coarse_lane, h, transposed):
    shape = (LANES, LANES)
    fine = lax.broadcasted_iota(jnp.int32, shape, 1 if transposed else 0) + h * LANES
    coarse = lax.broadcasted_iota(jnp.int32, shape, 0 if transposed else 1) + coarse_lane * LANES
    return jnp.where(fine // 2 == coarse, 1.0, 0.0).astype(jnp.bfloat16)


def exact_dot(a, ones):
    total = jnp.zeros((a.shape[0], ones.shape[1]), jnp.float32)
    parts = []
    for _ in range(3):
        part = a.astype(jnp.bfloat16)
        parts.append(part)
        a = a - part.astype(jnp.float32)
    for part in reversed(parts):
        total = total + jnp.dot(part, ones, preferred_element_type=jnp.float32)
    return total


def restrict_strips(read, halves, strips):
    rows = [
        jnp.concatenate([read(h, o) + read(h, o + 1) for o in range(0, strips, 2)], axis=0)
        for h in range(halves)
    ]
    result = []
    for c in range(halves // 2):
        tile = exact_dot(rows[2 * c], pairs(c, 2 * c, False))
        tile = tile + exact_dot(rows[2 * c + 1], pairs(c, 2 * c + 1, False))
        result.append(0.25 * tile)
    return result


def strips_of_perm(classes, table):
    ny, nz = classes.shape
    shape = strips_shape(ny, nz)

    def kernel(values, kinds, out, halves, sems):
        copies = halves_of(kinds, halves, sems)
        for copy in copies:
            copy.start()
        for h in range(shape[0]):
            copies[h].wait()
            for o in range(shape[1]):
                kind = strip(halves, h, o, shape[1])
                value = jnp.zeros((SUB, LANES), jnp.float32)
                for entry in range(table.shape[0]):
                    value = jnp.where(kind == entry, -ADV * values[entry], value)
                out[h, o] = value

    return pl.pallas_call(
        kernel,
        out_shape=jax.ShapeDtypeStruct(shape, jnp.float32),
        in_specs=in_smem(1) + anywhere(1),
        out_specs=in_vmem(1)[0],
        scratch_shapes=[pltpu.VMEM((shape[0], ny, LANES), jnp.int32),
                        pltpu.SemaphoreType.DMA((shape[0],))],
        compiler_params=small_vmem(),
        name="strips_of_perm",
    )(table, classes)


def strips_of_state(planes):
    count = len(planes)
    ny, nz = planes[0].shape
    halves_count, strips = nz // LANES, ny // SUB

    def kernel(*refs):
        outs, halves, sems = refs[count:2 * count], refs[2 * count], refs[2 * count + 1]
        copies = [halves_of(refs[i], halves.at[i], sems.at[i]) for i in range(count)]
        for row in copies:
            for copy in row:
                copy.start()
        for i in range(count):
            for h in range(halves_count):
                copies[i][h].wait()
                for o in range(strips):
                    value = strip(halves.at[i], h, o, strips)
                    outs[i][h, o + 1] = value
                    if o == 0:
                        outs[i][h, strips + 1] = pltpu.roll(value, SUB - 1, 0)
                    if o == strips - 1:
                        outs[i][h, 0] = pltpu.roll(value, 1, 0)

    return pl.pallas_call(
        kernel,
        out_shape=[jax.ShapeDtypeStruct(strips_shape(ny, nz, 2), jnp.float32)] * count,
        in_specs=anywhere(count),
        out_specs=in_vmem(count),
        scratch_shapes=[pltpu.VMEM((count, halves_count, ny, LANES), jnp.float32),
                        pltpu.SemaphoreType.DMA((count, halves_count))],
        compiler_params=small_vmem(),
        name="strips_of_state",
    )(*planes)


def coarse_parts(state, classes, rate_table):
    ny, nz = state.shape
    halves_count, strips = nz // LANES, ny // SUB
    coarse = (nz // (2 * LANES), ny // 2, LANES)

    def kernel(rates, field, kinds, own, ratio, fields_in, kinds_in, sems):
        copies = halves_of(field, fields_in, sems.at[0]) + halves_of(kinds, kinds_in, sems.at[1])
        for copy in copies:
            copy.start()
        for copy in copies:
            copy.wait()

        def rate(h, o):
            kind = strip(kinds_in, h, o, strips)
            value = jnp.zeros((SUB, LANES), jnp.float32)
            for entry in range(rate_table.shape[0]):
                value = jnp.where(kind == entry, rates[entry], value)
            return value

        for c, tile in enumerate(restrict_strips(rate, halves_count, strips)):
            ratio[c] = 1.0 / (1.0 + tile)
        read = lambda h, o: strip(fields_in, h, o, strips)
        for c, tile in enumerate(restrict_strips(read, halves_count, strips)):
            own[c] = tile

    return pl.pallas_call(
        kernel,
        out_shape=[jax.ShapeDtypeStruct(coarse, jnp.float32)] * 2,
        in_specs=in_smem(1) + anywhere(2),
        out_specs=in_vmem(2),
        scratch_shapes=[pltpu.VMEM((halves_count, ny, LANES), jnp.float32),
                        pltpu.VMEM((halves_count, ny, LANES), jnp.int32),
                        pltpu.SemaphoreType.DMA((2, halves_count))],
        compiler_params=small_vmem(),
        name="coarse_parts",
    )(rate_table, state, classes)


def gram_steps(g00, g01, g11, g12, g22, h22):
    a = 1.0 + 6.0 * DIFF
    b = 6.0 * DIFF
    g02 = 2.0 * g11 - g00
    h00, h01, h02 = g01, g11, g12
    h11, h12 = 0.5 * (g12 + g01), 0.5 * (g22 + g02)
    rr = g00
    alpha0 = rr / (a * g00 - b * h00)
    p, q = 1.0 - a * alpha0, b * alpha0
    new = p * p * g00 + 2.0 * p * q * g01 + q * q * g11
    beta = new / rr
    rr = new
    e, f = p + beta, q
    dd = e * e * g00 + 2.0 * e * f * g01 + f * f * g11
    dmd = e * e * h00 + 2.0 * e * f * h01 + f * f * h11
    alpha1 = rr / (a * dd - b * dmd)
    u = p - alpha1 * (a * e - 0.5 * b * f)
    v = q - alpha1 * (a * f - b * e)
    w = alpha1 * (0.5 * b) * f
    new = (u * u * g00 + v * v * g11 + w * w * g22
           + 2.0 * (u * v * g01 + u * w * g02 + v * w * g12))
    beta = new / rr
    rr = new
    u, v = u + beta * e, v + beta * f
    dd = (u * u * g00 + v * v * g11 + w * w * g22
          + 2.0 * (u * v * g01 + u * w * g02 + v * w * g12))
    dmd = (u * u * h00 + v * v * h11 + w * w * h22
           + 2.0 * (u * v * h01 + u * w * h02 + v * w * h12))
    alpha2 = rr / (a * dd - b * dmd)
    return (alpha0 + alpha1 * e + alpha2 * u, alpha1 * f + alpha2 * v, alpha2 * w)


def fine_kernel(planes, halves, strips):
    def kernel(*refs):
        x_in = refs[:planes]
        perm = refs[planes:2 * planes]
        outs = refs[2 * planes:3 * planes]
        x_next, r, p1, p2 = refs[3 * planes:]
        lane = lax.broadcasted_iota(jnp.int32, (DEPTH, SUB, LANES), 2)
        first_lane, last_lane = lane == 0, lane == LANES - 1
        zero = jnp.zeros((SUB, LANES), jnp.float32)
        cells = [(i, h) for i in range(planes) for h in range(halves)]

        def wrap(field):
            for i, h in cells:
                field[i, h, 0] = pltpu.roll(field[i, h, strips], 1, 0)
                field[i, h, strips + 1] = pltpu.roll(field[i, h, 1], SUB - 1, 0)

        def folded(value):
            return jnp.sum(value, axis=0)

        def total(acc):
            return jnp.sum(jnp.sum(acc, axis=1, keepdims=True), axis=0, keepdims=True)

        def uppers(row):
            turned = [pltpu.roll(c, LANES - 1, 2) for c in row]
            ends = turned[1:] + [jnp.zeros_like(row[0])]
            return [jnp.where(last_lane, e, t) for t, e in zip(turned, ends)]

        def lowers(row):
            turned = [pltpu.roll(c, 1, 2) for c in row]
            ends = [jnp.zeros_like(row[0])] + turned[:-1]
            return [jnp.where(first_lane, e, t) for t, e in zip(turned, ends)]

        def beside_planes(column):
            if planes == 4:
                even, odd = column[0] + column[2], column[1] + column[3]
                return [odd, even, odd, even]
            return [column[i - 1] + column[(i + 1) % planes] for i in range(planes)]

        def stencil(field, o):
            blocks = [[field[i][h, pl.ds(o, DEPTH + 2)] for h in range(halves)]
                      for i in range(planes)]
            inner = [[b[1:DEPTH + 1] for b in row] for row in blocks]
            along_x = [beside_planes([inner[i][h] for i in range(planes)]) for h in range(halves)]
            for i in range(planes):
                upper, lower = uppers(inner[i]), lowers(inner[i])
                for h in range(halves):
                    b = blocks[i][h]
                    six = (along_x[h][i] + (b[2:] + b[:DEPTH])) + (upper[h] + lower[h])
                    yield i, h, inner[i][h], six, upper[h], lower[h]

        def sweep(turn, init):
            carry = init
            for o in range(0, strips, DEPTH):
                carry = turn(o, carry)
            return carry

        def planes_of(field):
            return [field.at[i] for i in range(planes)]

        for step in range(FINE):
            last = step == FINE - 1
            x = x_in if step == 0 else planes_of(x_next)

            def first_pass(o, g00):
                for i, h, v, six, upper, lower in stencil(x, o):
                    slope = perm[i][h, pl.ds(o, DEPTH)] * (upper - lower) - 6.0 * DIFF
                    value = DIFF * six + slope * v
                    r[i, h, pl.ds(o + 1, DEPTH)] = value
                    g00 = g00 + folded(value * value)
                return g00

            g00 = sweep(first_pass, zero)
            wrap(r)

            def second_pass(o, carry):
                g01, g11 = carry
                for i, h, v, six, _, _ in stencil(planes_of(r), o):
                    value = six * (1.0 / 6.0)
                    p1[i, h, pl.ds(o + 1, DEPTH)] = value
                    g01 = g01 + folded(value * v)
                    g11 = g11 + folded(value * value)
                return g01, g11

            g01, g11 = sweep(second_pass, (zero, zero))
            wrap(p1)

            def third_pass(o, carry):
                g12, g22 = carry
                for i, h, v, six, _, _ in stencil(planes_of(p1), o):
                    value = six * (1.0 / 3.0) - r[i, h, pl.ds(o + 1, DEPTH)]
                    p2[i, h, pl.ds(o + 1, DEPTH)] = value
                    g12 = g12 + folded(value * v)
                    g22 = g22 + folded(value * value)
                return g12, g22

            g12, g22 = sweep(third_pass, (zero, zero))
            wrap(p2)

            def fourth_pass(o, h22):
                rows = []
                for i in range(planes):
                    blocks = [p2[i, h, pl.ds(o + 1, DEPTH + 1)] for h in range(halves)]
                    inner = [b[:DEPTH] for b in blocks]
                    rows.append(inner)
                    upper = uppers(inner)
                    for h in range(halves):
                        h22 = h22 + folded(inner[h] * (blocks[h][1:] + upper[h]))
                for h in range(halves):
                    if planes == 4:
                        h22 = h22 + folded((rows[0][h] + rows[2][h]) * (rows[1][h] + rows[3][h]))
                    else:
                        for i in range(planes):
                            h22 = h22 + folded(rows[i][h] * rows[(i + 1) % planes][h])
                return h22

            h22 = sweep(fourth_pass, zero)
            weights = gram_steps(
                total(g00), total(g01), total(g11), total(g12), total(g22),
                total(h22) * (1.0 / 3.0))
            c0, c1, c2 = (jnp.broadcast_to(c, (DEPTH, SUB, LANES)) for c in weights)

            def last_pass(o, carry):
                for i, h in cells:
                    at = pl.ds(o + 1, DEPTH)
                    value = (x[i][h, at] + c0 * r[i, h, at]) + (c1 * p1[i, h, at] + c2 * p2[i, h, at])
                    if last:
                        outs[i][h, pl.ds(o, DEPTH)] = value
                    else:
                        x_next[i, h, at] = value
                return carry

            sweep(last_pass, 0)
            if not last:
                wrap(x_next)

    return kernel


def fine_steps(state_strips, perm_strips):
    planes = len(state_strips)
    halves, strips = perm_strips[0].shape[:2]
    field = pltpu.VMEM((planes,) + state_strips[0].shape, jnp.float32)
    return pl.pallas_call(
        fine_kernel(planes, halves, strips),
        out_shape=[jax.ShapeDtypeStruct(perm_strips[0].shape, jnp.float32)] * planes,
        in_specs=in_vmem(2 * planes),
        out_specs=in_vmem(planes),
        scratch_shapes=[field] * 4,
        compiler_params=small_vmem(),
        name="fine_steps",
    )(*state_strips, *perm_strips)


def chosen(which, candidates, h, o):
    value = candidates[0][h, o]
    for k in range(1, len(candidates)):
        value = jnp.where(which == k, candidates[k][h, o], value)
    return value


def coarse_change(which, candidates, own):
    count = len(candidates)
    halves, strips = candidates[0].shape[:2]

    def kernel(choice, *refs):
        ends, own_ref, out = refs[:count], refs[count], refs[count + 1]
        read = lambda h, o: chosen(choice[0], ends, h, o)
        for c, tile in enumerate(restrict_strips(read, halves, strips)):
            out[c] = tile - own_ref[c]

    return pl.pallas_call(
        kernel,
        out_shape=jax.ShapeDtypeStruct(own.shape, jnp.float32),
        in_specs=in_smem(1) + in_vmem(count + 1),
        out_specs=in_vmem(1)[0],
        compiler_params=small_vmem(),
        name="coarse_change",
    )(which, *candidates, own)


def corrected(choice, candidates, ratio, changes, start):
    ny, nz = start.shape
    count, turns = len(candidates), len(changes)
    halves_count, strips = nz // LANES, ny // SUB

    def kernel(which, *refs):
        ends, share = refs[:count], refs[count]
        others = refs[count + 1:count + 1 + turns]
        begin, out, halves, sems = refs[count + 1 + turns:]

        @pl.when(which[1] == 0)
        def _():
            copy = pltpu.make_async_copy(begin, out, sems.at[0])
            copy.start()
            copy.wait()

        @pl.when(which[1] != 0)
        def _():
            copies = []
            for c in range(halves_count // 2):
                drift = jnp.zeros((ny // 2, LANES), jnp.float32)
                for k in reversed(range(turns)):
                    drift = share[c] * (drift + others[k][c])
                for h in (2 * c, 2 * c + 1):
                    wide = exact_dot(drift, pairs(c, h, True))
                    for o in range(strips):
                        first = (o // 2) * SUB
                        value = chosen(which[0], ends, h, o) + wide[first:first + SUB]
                        halves[h, pl.ds(o, SUB, stride=strips)] = value
                    copy = pltpu.make_async_copy(
                        halves.at[h], out.at[:, pl.ds(h * LANES, LANES)], sems.at[h])
                    copy.start()
                    copies.append(copy)
            for copy in copies:
                copy.wait()

    return pl.pallas_call(
        kernel,
        out_shape=jax.ShapeDtypeStruct((ny, nz), jnp.float32),
        in_specs=in_smem(1) + in_vmem(count + 1 + turns) + anywhere(1),
        out_specs=anywhere(1)[0],
        scratch_shapes=[pltpu.VMEM((halves_count, ny, LANES), jnp.float32),
                        pltpu.SemaphoreType.DMA((halves_count,))],
        compiler_params=small_vmem(),
        name="corrected",
    )(choice, *candidates, ratio, *changes, start)


def gathered_body(state, classes, perm_table, rate_table):
    start = state[0, 0]
    kinds = classes[0]
    width, slices = lax.axis_size("space"), lax.axis_size("tm")
    axes = ("space", "tm")
    place = lambda s, t: (s % width) * slices + t
    site = lambda j: (width // 2 - 1 + j % 2) % width
    used = range(slices - 1)
    far_first = sorted(range(1, width), key=lambda k: -min(k, width - k))

    def to_sites(array, k, late):
        return lax.ppermute(array, axes, [
            (place(site(j) + k, j + late), place(site(j), j + 1)) for j in used])

    def from_sites(array, k):
        return lax.ppermute(array, axes, [
            (place(site(j), j + 1), place(site(j) + k, j + 1)) for j in used])

    state_planes = {k: to_sites(start, k, 0) for k in far_first + [0]}
    perm = strips_of_perm(kinds, perm_table)
    perm_strips = {k: to_sites(perm, k, 1) for k in far_first}
    perm_strips[0] = perm
    own, ratio = coarse_parts(start, kinds, rate_table)
    state_strips = strips_of_state([state_planes[k] for k in range(width)])
    ends = fine_steps(state_strips, [perm_strips[k] for k in range(width)])
    landed = {k: from_sites(ends[k], k) for k in far_first}
    landed[0] = ends[0]
    candidates = [landed[k] for k in range(width)]
    turn = lax.axis_index("tm")
    which = (lax.axis_index("space") - site(turn - 1)) % width
    choice = jnp.stack([which, turn]).astype(jnp.int32)
    change = coarse_change(choice, candidates, own)
    changes = [
        lax.ppermute(change, "tm", [(i, i + k) for i in range(1, slices - k)])
        for k in range(1, slices - 1)
    ]
    return corrected(choice, candidates, ratio, changes, start)[None, None]


def body(state, classes, perm_table, rate_table):
    width = lax.axis_size("space")
    one_plane = state.shape[:2] == (1, 1) and classes.shape[0] == 1
    ny, nz = state.shape[2:]
    tiles = ny % (2 * DEPTH * SUB) == 0 and nz % (2 * LANES) == 0
    if one_plane and tiles and 2 < width <= MOST_PLANES and lax.axis_size("tm") > 2:
        return gathered_body(state, classes, perm_table, rate_table)
    return spread_body(state, classes, perm_table, rate_table)


def solution(mesh):
    placed = (
        P(("groups", "tm"), "space", None, None),
        P(("groups", "space"), None, None),
        P(),
        P(),
    )
    return jax.shard_map(
        body,
        mesh=mesh,
        in_specs=placed,
        out_specs=P(("groups", "tm"), "space", None, None),
        check_vma=False,
    )
```

```python
import jax
import jax.numpy as jnp
from jax import lax
from jax.experimental import pallas as pl
from jax.experimental.pallas import tpu as pltpu
from jax.sharding import PartitionSpec as P

ITERS = 3
FINE = 2


DIFF = 2.0
ADV = 0.25

SUB = 8
LANES = 128
DEPTH = 2
MOST_PLANES = 8
VMEM_BYTES = 16 * 1024 * 1024


def with_halo(array, sides, width):
    for axis, dim in sides:
        devices, length = (lax.axis_size(axis), array.shape[dim])
        up = [(i, (i + 1) % devices) for i in range(devices)]
        down = [(j, i) for i, j in up]
        last = lax.slice_in_dim(array, length - width, length, axis=dim)
        first = lax.slice_in_dim(array, 0, width, axis=dim)
        before = lax.ppermute(last, axis, up)
        after = lax.ppermute(first, axis, down)
        array = jnp.concatenate([before, array, after], axis=dim)
    return array


def passed_along(array, axis, by):
    devices = lax.axis_size(axis)
    pairs = [(i, i + by) for i in range(devices) if 0 <= i + by < devices]
    return lax.ppermute(array, axis, pairs)


def lookup(table, classes):
    values = jnp.zeros(classes.shape, jnp.float32)
    for entry in range(table.shape[0]):
        values = jnp.where(classes == entry, table[entry], values)
    return values


def restrict(field):
    cx, ny, nz = field.shape
    return field.reshape(cx, ny // 2, 2, nz // 2, 2).mean(axis=(2, 4))


def prolong(coarse):
    return jnp.repeat(jnp.repeat(coarse, 2, axis=1), 2, axis=2)


def vertical(field):
    zero_plane = jnp.zeros(field.shape[:2] + (1,), jnp.float32)
    upper = jnp.concatenate([field[:, :, 1:], zero_plane], axis=2)
    lower = jnp.concatenate([zero_plane, field[:, :, :-1]], axis=2)
    return (upper, lower)


def operate(field):
    padded = with_halo(field, (("space", 0),), 1)
    upper, lower = vertical(field)
    beside = padded[2:] + padded[:-2]
    beside = beside + jnp.roll(field, -1, 1) + jnp.roll(field, 1, 1)
    beside = beside + upper + lower
    return (1.0 + 6.0 * DIFF) * field - DIFF * beside


def squares(residual):
    return lax.psum(jnp.sum(residual * residual), "space")


def fine_step(field, perm):
    upper, lower = vertical(field)
    rhs = field - ADV * perm * field * (upper - lower)
    solution = field
    residual = rhs - operate(solution)
    direction = residual
    norm_now = squares(residual)
    for step in range(ITERS):
        image = operate(direction)
        alpha = norm_now / lax.psum(jnp.sum(direction * image), "space")
        solution = solution + alpha * direction
        residual = residual - alpha * image
        norm_next = squares(residual)
        direction = residual + norm_next / norm_now * direction
        norm_now = norm_next
    return solution


def spread_body(state, classes, perm_table, rate_table):
    start = state[0]
    perm = lookup(perm_table, classes)
    coarse_ratio = 1.0 / (1.0 + restrict(lookup(rate_table, classes)))
    field = start
    for step in range(FINE):
        field = fine_step(field, perm)
    coarse_start = restrict(start)
    jump = field - prolong(coarse_ratio * coarse_start)
    jump_coarse = restrict(jump)
    first = lax.axis_index("tm") == 0
    factor = jnp.where(first, 0.0, coarse_ratio)
    offset = jnp.where(first, coarse_ratio * coarse_start + jump_coarse, jump_coarse)
    before = passed_along(jump, "tm", 1)
    before_coarse = restrict(before)

    def relay_turn(turn, carry):
        outgoing, received = carry
        received = passed_along(outgoing, "tm", 1)
        return (factor * received + offset, received)

    outgoing, received = lax.fori_loop(
        0, lax.axis_size("tm") - 1, relay_turn, (offset, jnp.zeros_like(offset))
    )
    updated = jnp.where(first, start, before + prolong(received - before_coarse))
    return updated[None]


def in_vmem(count):
    return [pl.BlockSpec(memory_space=pltpu.VMEM)] * count


def anywhere(count):
    return [pl.BlockSpec(memory_space=pl.ANY)] * count


def in_hbm(count):
    return [pl.BlockSpec(memory_space=pltpu.HBM)] * count


def in_smem(count):
    return [pl.BlockSpec(memory_space=pltpu.SMEM)] * count


def small_vmem():
    return pltpu.CompilerParams(vmem_limit_bytes=VMEM_BYTES)


def strips_shape(ny, nz, extra=0):
    return (nz // LANES, ny // SUB + extra, SUB, LANES)


def halves_of(plane, halves, sems):
    return [
        pltpu.make_async_copy(plane.at[:, pl.ds(h * LANES, LANES)], halves.at[h], sems.at[h])
        for h in range(halves.shape[0])
    ]


def strip(halves, h, o, strips):
    return halves[h, pl.ds(o, SUB, stride=strips)]


def pairs(coarse_lane, h, transposed):
    shape = (LANES, LANES)
    fine = lax.broadcasted_iota(jnp.int32, shape, 1 if transposed else 0) + h * LANES
    coarse = lax.broadcasted_iota(jnp.int32, shape, 0 if transposed else 1) + coarse_lane * LANES
    return jnp.where(fine // 2 == coarse, 1.0, 0.0).astype(jnp.bfloat16)


def exact_dot(a, ones):
    total = jnp.zeros((a.shape[0], ones.shape[1]), jnp.float32)
    parts = []
    for _ in range(3):
        part = a.astype(jnp.bfloat16)
        parts.append(part)
        a = a - part.astype(jnp.float32)
    for part in reversed(parts):
        total = total + jnp.dot(part, ones, preferred_element_type=jnp.float32)
    return total


def restrict_strips(read, halves, strips):
    rows = [
        jnp.concatenate([read(h, o) + read(h, o + 1) for o in range(0, strips, 2)], axis=0)
        for h in range(halves)
    ]
    result = []
    for c in range(halves // 2):
        tile = exact_dot(rows[2 * c], pairs(c, 2 * c, False))
        tile = tile + exact_dot(rows[2 * c + 1], pairs(c, 2 * c + 1, False))
        result.append(0.25 * tile)
    return result


def strips_of_perm(classes, table):
    ny, nz = classes.shape
    shape = strips_shape(ny, nz)

    def kernel(values, kinds, out, halves, sems):
        copies = halves_of(kinds, halves, sems)
        for copy in copies:
            copy.start()
        for h in range(shape[0]):
            copies[h].wait()
            for o in range(shape[1]):
                kind = strip(halves, h, o, shape[1])
                value = jnp.zeros((SUB, LANES), jnp.float32)
                for entry in range(table.shape[0]):
                    value = jnp.where(kind == entry, -ADV * values[entry], value)
                out[h, o] = value

    return pl.pallas_call(
        kernel,
        out_shape=jax.ShapeDtypeStruct(shape, jnp.float32),
        in_specs=in_smem(1) + in_hbm(1),
        out_specs=in_vmem(1)[0],
        scratch_shapes=[pltpu.VMEM((shape[0], ny, LANES), jnp.int32),
                        pltpu.SemaphoreType.DMA((shape[0],))],
        compiler_params=small_vmem(),
        name="strips_of_perm",
    )(table, classes)


def strips_of_state(planes):
    count = len(planes)
    ny, nz = planes[0].shape
    halves_count, strips = nz // LANES, ny // SUB

    def kernel(*refs):
        outs, halves, sems = refs[count:2 * count], refs[2 * count], refs[2 * count + 1]
        copies = [halves_of(refs[i], halves.at[i], sems.at[i]) for i in range(count)]
        for row in copies:
            for copy in row:
                copy.start()
        for i in range(count):
            for h in range(halves_count):
                copies[i][h].wait()
                for o in range(strips):
                    value = strip(halves.at[i], h, o, strips)
                    outs[i][h, o + 1] = value
                    if o == 0:
                        outs[i][h, strips + 1] = pltpu.roll(value, SUB - 1, 0)
                    if o == strips - 1:
                        outs[i][h, 0] = pltpu.roll(value, 1, 0)

    return pl.pallas_call(
        kernel,
        out_shape=[jax.ShapeDtypeStruct(strips_shape(ny, nz, 2), jnp.float32)] * count,
        in_specs=anywhere(count),
        out_specs=in_vmem(count),
        scratch_shapes=[pltpu.VMEM((count, halves_count, ny, LANES), jnp.float32),
                        pltpu.SemaphoreType.DMA((count, halves_count))],
        compiler_params=small_vmem(),
        name="strips_of_state",
    )(*planes)


def coarse_parts(state, classes, rate_table):
    ny, nz = state.shape
    halves_count, strips = nz // LANES, ny // SUB
    coarse = (nz // (2 * LANES), ny // 2, LANES)

    def kernel(rates, field, kinds, own, ratio, fields_in, kinds_in, sems):
        copies = halves_of(field, fields_in, sems.at[0]) + halves_of(kinds, kinds_in, sems.at[1])
        for copy in copies:
            copy.start()
        for copy in copies:
            copy.wait()

        def rate(h, o):
            kind = strip(kinds_in, h, o, strips)
            value = jnp.zeros((SUB, LANES), jnp.float32)
            for entry in range(rate_table.shape[0]):
                value = jnp.where(kind == entry, rates[entry], value)
            return value

        for c, tile in enumerate(restrict_strips(rate, halves_count, strips)):
            ratio[c] = 1.0 / (1.0 + tile)
        read = lambda h, o: strip(fields_in, h, o, strips)
        for c, tile in enumerate(restrict_strips(read, halves_count, strips)):
            own[c] = tile

    return pl.pallas_call(
        kernel,
        out_shape=[jax.ShapeDtypeStruct(coarse, jnp.float32)] * 2,
        in_specs=in_smem(1) + in_hbm(2),
        out_specs=in_vmem(2),
        scratch_shapes=[pltpu.VMEM((halves_count, ny, LANES), jnp.float32),
                        pltpu.VMEM((halves_count, ny, LANES), jnp.int32),
                        pltpu.SemaphoreType.DMA((2, halves_count))],
        compiler_params=small_vmem(),
        name="coarse_parts",
    )(rate_table, pltpu.with_memory_space_constraint(state, pltpu.HBM), pltpu.with_memory_space_constraint(classes, pltpu.HBM))


def gram_steps(g00, g01, g11, g12, g22, h22):
    a = 1.0 + 6.0 * DIFF
    b = 6.0 * DIFF
    g02 = 2.0 * g11 - g00
    h00, h01, h02 = g01, g11, g12
    h11, h12 = 0.5 * (g12 + g01), 0.5 * (g22 + g02)
    rr = g00
    alpha0 = rr / (a * g00 - b * h00)
    p, q = 1.0 - a * alpha0, b * alpha0
    new = p * p * g00 + 2.0 * p * q * g01 + q * q * g11
    beta = new / rr
    rr = new
    e, f = p + beta, q
    dd = e * e * g00 + 2.0 * e * f * g01 + f * f * g11
    dmd = e * e * h00 + 2.0 * e * f * h01 + f * f * h11
    alpha1 = rr / (a * dd - b * dmd)
    u = p - alpha1 * (a * e - 0.5 * b * f)
    v = q - alpha1 * (a * f - b * e)
    w = alpha1 * (0.5 * b) * f
    new = (u * u * g00 + v * v * g11 + w * w * g22
           + 2.0 * (u * v * g01 + u * w * g02 + v * w * g12))
    beta = new / rr
    rr = new
    u, v = u + beta * e, v + beta * f
    dd = (u * u * g00 + v * v * g11 + w * w * g22
          + 2.0 * (u * v * g01 + u * w * g02 + v * w * g12))
    dmd = (u * u * h00 + v * v * h11 + w * w * h22
           + 2.0 * (u * v * h01 + u * w * h02 + v * w * h12))
    alpha2 = rr / (a * dd - b * dmd)
    return (alpha0 + alpha1 * e + alpha2 * u, alpha1 * f + alpha2 * v, alpha2 * w)


def fine_kernel(order, halves, strips):
    planes = len(order)

    def kernel(active, *refs):
        @pl.when(active[0] == 1)
        def _():
            steps(*refs)

    def steps(*refs):
        x_in = [refs[order.index(k)] for k in range(planes)]
        perm = [refs[planes + order.index(k)] for k in range(planes)]
        outs = refs[2 * planes:3 * planes]
        x_next, r, p1, p2 = refs[3 * planes:]
        lane = lax.broadcasted_iota(jnp.int32, (DEPTH, SUB, LANES), 2)
        first_lane, last_lane = lane == 0, lane == LANES - 1
        zero = jnp.zeros((SUB, LANES), jnp.float32)
        cells = [(i, h) for i in range(planes) for h in range(halves)]

        def wrap(field):
            for i, h in cells:
                field[i, h, 0] = pltpu.roll(field[i, h, strips], 1, 0)
                field[i, h, strips + 1] = pltpu.roll(field[i, h, 1], SUB - 1, 0)

        def folded(value):
            return jnp.sum(value, axis=0)

        def total(acc):
            return jnp.sum(jnp.sum(acc, axis=1, keepdims=True), axis=0, keepdims=True)

        def uppers(row):
            turned = [pltpu.roll(c, LANES - 1, 2) for c in row]
            ends = turned[1:] + [jnp.zeros_like(row[0])]
            return [jnp.where(last_lane, e, t) for t, e in zip(turned, ends)]

        def lowers(row):
            turned = [pltpu.roll(c, 1, 2) for c in row]
            ends = [jnp.zeros_like(row[0])] + turned[:-1]
            return [jnp.where(first_lane, e, t) for t, e in zip(turned, ends)]

        def beside_planes(column):
            if planes == 4:
                even, odd = column[0] + column[2], column[1] + column[3]
                return [odd, even, odd, even]
            return [column[i - 1] + column[(i + 1) % planes] for i in range(planes)]

        def stencil(field, o):
            blocks = [[field[i][h, pl.ds(o, DEPTH + 2)] for h in range(halves)]
                      for i in range(planes)]
            inner = [[b[1:DEPTH + 1] for b in row] for row in blocks]
            along_x = [beside_planes([inner[i][h] for i in range(planes)]) for h in range(halves)]
            for i in range(planes):
                upper, lower = uppers(inner[i]), lowers(inner[i])
                for h in range(halves):
                    b = blocks[i][h]
                    six = (along_x[h][i] + (b[2:] + b[:DEPTH])) + (upper[h] + lower[h])
                    yield i, h, inner[i][h], six, upper[h], lower[h]

        def sweep(turn, init):
            carry = init
            for o in range(0, strips, DEPTH):
                carry = turn(o, carry)
            return carry

        def planes_of(field):
            return [field.at[i] for i in range(planes)]

        for step in range(FINE):
            last = step == FINE - 1
            x = x_in if step == 0 else planes_of(x_next)

            def first_pass(o, g00):
                for i, h, v, six, upper, lower in stencil(x, o):
                    slope = perm[i][h, pl.ds(o, DEPTH)] * (upper - lower) - 6.0 * DIFF
                    value = DIFF * six + slope * v
                    r[i, h, pl.ds(o + 1, DEPTH)] = value
                    g00 = g00 + folded(value * value)
                return g00

            g00 = sweep(first_pass, zero)
            wrap(r)

            def second_pass(o, carry):
                g01, g11 = carry
                for i, h, v, six, _, _ in stencil(planes_of(r), o):
                    value = six * (1.0 / 6.0)
                    p1[i, h, pl.ds(o + 1, DEPTH)] = value
                    g01 = g01 + folded(value * v)
                    g11 = g11 + folded(value * value)
                return g01, g11

            g01, g11 = sweep(second_pass, (zero, zero))
            wrap(p1)

            def third_pass(o, carry):
                g12, g22 = carry
                for i, h, v, six, _, _ in stencil(planes_of(p1), o):
                    value = six * (1.0 / 3.0) - r[i, h, pl.ds(o + 1, DEPTH)]
                    p2[i, h, pl.ds(o + 1, DEPTH)] = value
                    g12 = g12 + folded(value * v)
                    g22 = g22 + folded(value * value)
                return g12, g22

            g12, g22 = sweep(third_pass, (zero, zero))
            wrap(p2)

            def fourth_pass(o, h22):
                rows = []
                for i in range(planes):
                    blocks = [p2[i, h, pl.ds(o + 1, DEPTH + 1)] for h in range(halves)]
                    inner = [b[:DEPTH] for b in blocks]
                    rows.append(inner)
                    upper = uppers(inner)
                    for h in range(halves):
                        h22 = h22 + folded(inner[h] * (blocks[h][1:] + upper[h]))
                for h in range(halves):
                    if planes == 4:
                        h22 = h22 + folded((rows[0][h] + rows[2][h]) * (rows[1][h] + rows[3][h]))
                    else:
                        for i in range(planes):
                            h22 = h22 + folded(rows[i][h] * rows[(i + 1) % planes][h])
                return h22

            h22 = sweep(fourth_pass, zero)
            weights = gram_steps(
                total(g00), total(g01), total(g11), total(g12), total(g22),
                total(h22) * (1.0 / 3.0))
            c0, c1, c2 = (jnp.broadcast_to(c, (DEPTH, SUB, LANES)) for c in weights)

            def last_pass(o, carry):
                for i, h in cells:
                    at = pl.ds(o + 1, DEPTH)
                    value = (x[i][h, at] + c0 * r[i, h, at]) + (c1 * p1[i, h, at] + c2 * p2[i, h, at])
                    if last:
                        outs[i][h, pl.ds(o, DEPTH)] = value
                    else:
                        x_next[i, h, at] = value
                return carry

            sweep(last_pass, 0)
            if not last:
                wrap(x_next)

    return kernel


def fine_steps(active, state_strips, perm_strips, order):
    planes = len(order)
    shape = perm_strips[0].shape
    field = pltpu.VMEM((planes,) + state_strips[0].shape, jnp.float32)
    return pl.pallas_call(
        fine_kernel(order, *shape[:2]),
        out_shape=[jax.ShapeDtypeStruct(shape, jnp.float32)] * planes,
        in_specs=in_smem(1) + in_vmem(2 * planes),
        out_specs=in_vmem(planes),
        scratch_shapes=[field] * 4,
        compiler_params=small_vmem(),
        name="fine_steps",
    )(active, *[state_strips[k] for k in order], *[perm_strips[k] for k in order])


def chosen(which, candidates, h, o):
    value = candidates[0][h, o]
    for k in range(1, len(candidates)):
        value = jnp.where(which == k, candidates[k][h, o], value)
    return value


def coarse_change(which, candidates, own):
    count = len(candidates)
    halves, strips = candidates[0].shape[:2]

    def kernel(choice, *refs):
        ends, own_ref, out = refs[:count], refs[count], refs[count + 1]
        read = lambda h, o: chosen(choice[0], ends, h, o)
        for c, tile in enumerate(restrict_strips(read, halves, strips)):
            out[c] = tile - own_ref[c]

    return pl.pallas_call(
        kernel,
        out_shape=jax.ShapeDtypeStruct(own.shape, jnp.float32),
        in_specs=in_smem(1) + in_vmem(count + 1),
        out_specs=in_vmem(1)[0],
        compiler_params=small_vmem(),
        name="coarse_change",
    )(which, *candidates, own)


def corrected(choice, candidates, ratio, changes, start):
    ny, nz = start.shape
    count, turns = len(candidates), len(changes)
    halves_count, strips = nz // LANES, ny // SUB

    def kernel(which, *refs):
        ends, share = refs[:count], refs[count]
        others = refs[count + 1:count + 1 + turns]
        begin, out, halves, sems = refs[count + 1 + turns:]

        @pl.when(which[1] == 0)
        def _():
            copy = pltpu.make_async_copy(begin, out, sems.at[0])
            copy.start()
            copy.wait()

        @pl.when(which[1] != 0)
        def _():
            copies = []
            for c in range(halves_count // 2):
                drift = jnp.zeros((ny // 2, LANES), jnp.float32)
                for k in reversed(range(turns)):
                    drift = share[c] * (drift + others[k][c])
                for h in (2 * c, 2 * c + 1):
                    wide = exact_dot(drift, pairs(c, h, True))
                    for o in range(strips):
                        first = (o // 2) * SUB
                        value = chosen(which[0], ends, h, o) + wide[first:first + SUB]
                        halves[h, pl.ds(o, SUB, stride=strips)] = value
                    copy = pltpu.make_async_copy(
                        halves.at[h], out.at[:, pl.ds(h * LANES, LANES)], sems.at[h])
                    copy.start()
                    copies.append(copy)
            for copy in copies:
                copy.wait()

    return pl.pallas_call(
        kernel,
        out_shape=jax.ShapeDtypeStruct((ny, nz), jnp.float32),
        in_specs=in_smem(1) + in_vmem(count + 1 + turns) + in_hbm(1),
        out_specs=in_hbm(1)[0],
        scratch_shapes=[pltpu.VMEM((halves_count, ny, LANES), jnp.float32),
                        pltpu.SemaphoreType.DMA((halves_count,))],
        compiler_params=small_vmem(),
        name="corrected",
    )(choice, *candidates, ratio, *changes, pltpu.with_memory_space_constraint(start, pltpu.HBM))


def gathered_body(state, classes, perm_table, rate_table):
    start = state[0, 0]
    kinds = classes[0]
    width, slices = lax.axis_size("space"), lax.axis_size("tm")
    axes = ("space", "tm")
    place = lambda s, t: (s % width) * slices + t
    site = lambda j: (width // 2 - 1 + j % 2) % width
    used = range(slices - 1)

    def to_sites(array, k):
        return lax.ppermute(array, axes, [
            (place(site(j) + k, j), place(site(j), j)) for j in used])

    def from_sites(array, k):
        return lax.ppermute(array, axes, [
            (place(site(j), j), place(site(j) + k, j + 1)) for j in used])

    order = sorted(range(1, width), key=lambda k: (min(k, width - k), -k)) + [0]
    state_planes = {k: to_sites(start, k) for k in order[:-1]}
    state_planes[0] = start
    perm = strips_of_perm(kinds, perm_table)
    perm_strips = {k: to_sites(perm, k) for k in order[:-1]}
    perm_strips[0] = perm
    own, ratio = coarse_parts(start, kinds, rate_table)
    state_strips = dict(zip(order, strips_of_state([state_planes[k] for k in order])))
    turn, plane = lax.axis_index("tm"), lax.axis_index("space")
    here = (turn < slices - 1) & (plane == site(turn))
    ends = fine_steps(here.astype(jnp.int32)[None], state_strips, perm_strips, order)
    candidates = [from_sites(ends[k], k) for k in range(width)]
    which = (plane - site(turn - 1)) % width
    choice = jnp.stack([which, turn]).astype(jnp.int32)
    change = coarse_change(choice, candidates, own)
    changes = [
        lax.ppermute(change, "tm", [(i, i + k) for i in range(1, slices - k)])
        for k in range(1, slices - 1)
    ]
    return corrected(choice, candidates, ratio, changes, start)[None, None]


def body(state, classes, perm_table, rate_table):
    width = lax.axis_size("space")
    one_plane = state.shape[:2] == (1, 1) and classes.shape[0] == 1
    ny, nz = state.shape[2:]
    tiles = ny % (2 * DEPTH * SUB) == 0 and nz % (2 * LANES) == 0
    if one_plane and tiles and 2 < width <= MOST_PLANES and lax.axis_size("tm") > 2:
        return gathered_body(state, classes, perm_table, rate_table)
    return spread_body(state, classes, perm_table, rate_table)


def solution(mesh):
    placed = (
        P(("groups", "tm"), "space", None, None),
        P(("groups", "space"), None, None),
        P(),
        P(),
    )
    return jax.shard_map(
        body,
        mesh=mesh,
        in_specs=placed,
        out_specs=P(("groups", "tm"), "space", None, None),
        check_vma=False,
    )
```

```python
import jax
import jax.numpy as jnp
from jax import lax
from jax.experimental import pallas as pl
from jax.experimental.pallas import tpu as pltpu
from jax.sharding import PartitionSpec as P

ITERS = 3
FINE = 2


DIFF = 2.0
ADV = 0.25

SUB = 8
LANES = 128
DEPTH = 2
MOST_PLANES = 8
VMEM_BYTES = 16 * 1024 * 1024


def with_halo(array, sides, width):
    for axis, dim in sides:
        devices, length = (lax.axis_size(axis), array.shape[dim])
        up = [(i, (i + 1) % devices) for i in range(devices)]
        down = [(j, i) for i, j in up]
        last = lax.slice_in_dim(array, length - width, length, axis=dim)
        first = lax.slice_in_dim(array, 0, width, axis=dim)
        before = lax.ppermute(last, axis, up)
        after = lax.ppermute(first, axis, down)
        array = jnp.concatenate([before, array, after], axis=dim)
    return array


def passed_along(array, axis, by):
    devices = lax.axis_size(axis)
    pairs = [(i, i + by) for i in range(devices) if 0 <= i + by < devices]
    return lax.ppermute(array, axis, pairs)


def lookup(table, classes):
    values = jnp.zeros(classes.shape, jnp.float32)
    for entry in range(table.shape[0]):
        values = jnp.where(classes == entry, table[entry], values)
    return values


def restrict(field):
    cx, ny, nz = field.shape
    return field.reshape(cx, ny // 2, 2, nz // 2, 2).mean(axis=(2, 4))


def prolong(coarse):
    return jnp.repeat(jnp.repeat(coarse, 2, axis=1), 2, axis=2)


def vertical(field):
    zero_plane = jnp.zeros(field.shape[:2] + (1,), jnp.float32)
    upper = jnp.concatenate([field[:, :, 1:], zero_plane], axis=2)
    lower = jnp.concatenate([zero_plane, field[:, :, :-1]], axis=2)
    return (upper, lower)


def operate(field):
    padded = with_halo(field, (("space", 0),), 1)
    upper, lower = vertical(field)
    beside = padded[2:] + padded[:-2]
    beside = beside + jnp.roll(field, -1, 1) + jnp.roll(field, 1, 1)
    beside = beside + upper + lower
    return (1.0 + 6.0 * DIFF) * field - DIFF * beside


def squares(residual):
    return lax.psum(jnp.sum(residual * residual), "space")


def fine_step(field, perm):
    upper, lower = vertical(field)
    rhs = field - ADV * perm * field * (upper - lower)
    solution = field
    residual = rhs - operate(solution)
    direction = residual
    norm_now = squares(residual)
    for step in range(ITERS):
        image = operate(direction)
        alpha = norm_now / lax.psum(jnp.sum(direction * image), "space")
        solution = solution + alpha * direction
        residual = residual - alpha * image
        norm_next = squares(residual)
        direction = residual + norm_next / norm_now * direction
        norm_now = norm_next
    return solution


def spread_body(state, classes, perm_table, rate_table):
    start = state[0]
    perm = lookup(perm_table, classes)
    coarse_ratio = 1.0 / (1.0 + restrict(lookup(rate_table, classes)))
    field = start
    for step in range(FINE):
        field = fine_step(field, perm)
    coarse_start = restrict(start)
    jump = field - prolong(coarse_ratio * coarse_start)
    jump_coarse = restrict(jump)
    first = lax.axis_index("tm") == 0
    factor = jnp.where(first, 0.0, coarse_ratio)
    offset = jnp.where(first, coarse_ratio * coarse_start + jump_coarse, jump_coarse)
    before = passed_along(jump, "tm", 1)
    before_coarse = restrict(before)

    def relay_turn(turn, carry):
        outgoing, received = carry
        received = passed_along(outgoing, "tm", 1)
        return (factor * received + offset, received)

    outgoing, received = lax.fori_loop(
        0, lax.axis_size("tm") - 1, relay_turn, (offset, jnp.zeros_like(offset))
    )
    updated = jnp.where(first, start, before + prolong(received - before_coarse))
    return updated[None]


def in_vmem(count):
    return [pl.BlockSpec(memory_space=pltpu.VMEM)] * count


def anywhere(count):
    return [pl.BlockSpec(memory_space=pl.ANY)] * count


def in_hbm(count):
    return [pl.BlockSpec(memory_space=pltpu.HBM)] * count


def in_smem(count):
    return [pl.BlockSpec(memory_space=pltpu.SMEM)] * count


def small_vmem():
    return pltpu.CompilerParams(vmem_limit_bytes=VMEM_BYTES)


def strips_shape(ny, nz, extra=0):
    return (nz // LANES, ny // SUB + extra, SUB, LANES)


def halves_of(plane, halves, sems):
    return [
        pltpu.make_async_copy(plane.at[:, pl.ds(h * LANES, LANES)], halves.at[h], sems.at[h])
        for h in range(halves.shape[0])
    ]


def strip(halves, h, o, strips):
    return halves[h, pl.ds(o, SUB, stride=strips)]


def pairs(coarse_lane, h, transposed):
    shape = (LANES, LANES)
    fine = lax.broadcasted_iota(jnp.int32, shape, 1 if transposed else 0) + h * LANES
    coarse = lax.broadcasted_iota(jnp.int32, shape, 0 if transposed else 1) + coarse_lane * LANES
    return jnp.where(fine // 2 == coarse, 1.0, 0.0).astype(jnp.bfloat16)


def exact_dot(a, ones):
    total = jnp.zeros((a.shape[0], ones.shape[1]), jnp.float32)
    parts = []
    for _ in range(3):
        part = a.astype(jnp.bfloat16)
        parts.append(part)
        a = a - part.astype(jnp.float32)
    for part in reversed(parts):
        total = total + jnp.dot(part, ones, preferred_element_type=jnp.float32)
    return total


def restrict_strips(read, halves, strips):
    rows = [
        jnp.concatenate([read(h, o) + read(h, o + 1) for o in range(0, strips, 2)], axis=0)
        for h in range(halves)
    ]
    result = []
    for c in range(halves // 2):
        tile = exact_dot(rows[2 * c], pairs(c, 2 * c, False))
        tile = tile + exact_dot(rows[2 * c + 1], pairs(c, 2 * c + 1, False))
        result.append(0.25 * tile)
    return result


def strips_of_perm(classes, table):
    ny, nz = classes.shape
    shape = strips_shape(ny, nz)

    def kernel(values, kinds, out, halves, sems):
        copies = halves_of(kinds, halves, sems)
        for copy in copies:
            copy.start()
        for h in range(shape[0]):
            copies[h].wait()
            for o in range(shape[1]):
                kind = strip(halves, h, o, shape[1])
                value = jnp.zeros((SUB, LANES), jnp.float32)
                for entry in range(table.shape[0]):
                    value = jnp.where(kind == entry, -ADV * values[entry], value)
                out[h, o] = value

    return pl.pallas_call(
        kernel,
        out_shape=jax.ShapeDtypeStruct(shape, jnp.float32),
        in_specs=in_smem(1) + in_hbm(1),
        out_specs=in_vmem(1)[0],
        scratch_shapes=[pltpu.VMEM((shape[0], ny, LANES), jnp.int32),
                        pltpu.SemaphoreType.DMA((shape[0],))],
        compiler_params=small_vmem(),
        name="strips_of_perm",
    )(table, classes)


def strips_of_state(planes):
    count = len(planes)
    ny, nz = planes[0].shape
    halves_count, strips = nz // LANES, ny // SUB

    def kernel(*refs):
        outs, halves, sems = refs[count:2 * count], refs[2 * count], refs[2 * count + 1]
        copies = [halves_of(refs[i], halves.at[i], sems.at[i]) for i in range(count)]
        for row in copies:
            for copy in row:
                copy.start()
        for i in range(count):
            for h in range(halves_count):
                copies[i][h].wait()
                for o in range(strips):
                    value = strip(halves.at[i], h, o, strips)
                    outs[i][h, o + 1] = value
                    if o == 0:
                        outs[i][h, strips + 1] = pltpu.roll(value, SUB - 1, 0)
                    if o == strips - 1:
                        outs[i][h, 0] = pltpu.roll(value, 1, 0)

    return pl.pallas_call(
        kernel,
        out_shape=[jax.ShapeDtypeStruct(strips_shape(ny, nz, 2), jnp.float32)] * count,
        in_specs=anywhere(count),
        out_specs=in_vmem(count),
        scratch_shapes=[pltpu.VMEM((count, halves_count, ny, LANES), jnp.float32),
                        pltpu.SemaphoreType.DMA((count, halves_count))],
        compiler_params=small_vmem(),
        name="strips_of_state",
    )(*planes)


def coarse_parts(state, classes, rate_table):
    ny, nz = state.shape
    halves_count, strips = nz // LANES, ny // SUB
    coarse = (nz // (2 * LANES), ny // 2, LANES)

    def kernel(rates, field, kinds, own, ratio, fields_in, kinds_in, sems):
        copies = halves_of(field, fields_in, sems.at[0]) + halves_of(kinds, kinds_in, sems.at[1])
        for copy in copies:
            copy.start()
        for copy in copies:
            copy.wait()

        def rate(h, o):
            kind = strip(kinds_in, h, o, strips)
            value = jnp.zeros((SUB, LANES), jnp.float32)
            for entry in range(rate_table.shape[0]):
                value = jnp.where(kind == entry, rates[entry], value)
            return value

        for c, tile in enumerate(restrict_strips(rate, halves_count, strips)):
            ratio[c] = 1.0 / (1.0 + tile)
        read = lambda h, o: strip(fields_in, h, o, strips)
        for c, tile in enumerate(restrict_strips(read, halves_count, strips)):
            own[c] = tile

    return pl.pallas_call(
        kernel,
        out_shape=[jax.ShapeDtypeStruct(coarse, jnp.float32)] * 2,
        in_specs=in_smem(1) + in_hbm(2),
        out_specs=in_vmem(2),
        scratch_shapes=[pltpu.VMEM((halves_count, ny, LANES), jnp.float32),
                        pltpu.VMEM((halves_count, ny, LANES), jnp.int32),
                        pltpu.SemaphoreType.DMA((2, halves_count))],
        compiler_params=small_vmem(),
        name="coarse_parts",
    )(rate_table, pltpu.with_memory_space_constraint(state, pltpu.HBM), pltpu.with_memory_space_constraint(classes, pltpu.HBM))


def gram_steps(g00, g01, g11, g12, g22, h22):
    a = 1.0 + 6.0 * DIFF
    b = 6.0 * DIFF
    g02 = 2.0 * g11 - g00
    h00, h01, h02 = g01, g11, g12
    h11, h12 = 0.5 * (g12 + g01), 0.5 * (g22 + g02)
    rr = g00
    alpha0 = rr / (a * g00 - b * h00)
    p, q = 1.0 - a * alpha0, b * alpha0
    new = p * p * g00 + 2.0 * p * q * g01 + q * q * g11
    beta = new / rr
    rr = new
    e, f = p + beta, q
    dd = e * e * g00 + 2.0 * e * f * g01 + f * f * g11
    dmd = e * e * h00 + 2.0 * e * f * h01 + f * f * h11
    alpha1 = rr / (a * dd - b * dmd)
    u = p - alpha1 * (a * e - 0.5 * b * f)
    v = q - alpha1 * (a * f - b * e)
    w = alpha1 * (0.5 * b) * f
    new = (u * u * g00 + v * v * g11 + w * w * g22
           + 2.0 * (u * v * g01 + u * w * g02 + v * w * g12))
    beta = new / rr
    rr = new
    u, v = u + beta * e, v + beta * f
    dd = (u * u * g00 + v * v * g11 + w * w * g22
          + 2.0 * (u * v * g01 + u * w * g02 + v * w * g12))
    dmd = (u * u * h00 + v * v * h11 + w * w * h22
           + 2.0 * (u * v * h01 + u * w * h02 + v * w * h12))
    alpha2 = rr / (a * dd - b * dmd)
    return (alpha0 + alpha1 * e + alpha2 * u, alpha1 * f + alpha2 * v, alpha2 * w)


def fine_kernel(order, halves, strips):
    planes = len(order)

    def kernel(active, *refs):
        @pl.when(active[0] == 1)
        def _():
            steps(*refs)

    def steps(*refs):
        x_in = [refs[order.index(k)] for k in range(planes)]
        perm = [refs[planes + order.index(k)] for k in range(planes)]
        outs = refs[2 * planes:3 * planes]
        x_next, r, p1, p2 = refs[3 * planes:]
        lane = lax.broadcasted_iota(jnp.int32, (DEPTH, SUB, LANES), 2)
        first_lane, last_lane = lane == 0, lane == LANES - 1
        zero = jnp.zeros((SUB, LANES), jnp.float32)
        cells = [(i, h) for i in range(planes) for h in range(halves)]

        def wrap(field):
            for i, h in cells:
                field[i, h, 0] = pltpu.roll(field[i, h, strips], 1, 0)
                field[i, h, strips + 1] = pltpu.roll(field[i, h, 1], SUB - 1, 0)

        def folded(value):
            return jnp.sum(value, axis=0)

        def total(acc):
            return jnp.sum(jnp.sum(acc, axis=1, keepdims=True), axis=0, keepdims=True)

        def uppers(row):
            turned = [pltpu.roll(c, LANES - 1, 2) for c in row]
            ends = turned[1:] + [jnp.zeros_like(row[0])]
            return [jnp.where(last_lane, e, t) for t, e in zip(turned, ends)]

        def lowers(row):
            turned = [pltpu.roll(c, 1, 2) for c in row]
            ends = [jnp.zeros_like(row[0])] + turned[:-1]
            return [jnp.where(first_lane, e, t) for t, e in zip(turned, ends)]

        def beside_planes(column):
            if planes == 4:
                even, odd = column[0] + column[2], column[1] + column[3]
                return [odd, even, odd, even]
            return [column[i - 1] + column[(i + 1) % planes] for i in range(planes)]

        def stencil(field, o):
            blocks = [[field[i][h, pl.ds(o, DEPTH + 2)] for h in range(halves)]
                      for i in range(planes)]
            inner = [[b[1:DEPTH + 1] for b in row] for row in blocks]
            along_x = [beside_planes([inner[i][h] for i in range(planes)]) for h in range(halves)]
            for i in range(planes):
                upper, lower = uppers(inner[i]), lowers(inner[i])
                for h in range(halves):
                    b = blocks[i][h]
                    six = (along_x[h][i] + (b[2:] + b[:DEPTH])) + (upper[h] + lower[h])
                    yield i, h, inner[i][h], six, upper[h], lower[h]

        def sweep(turn, init):
            carry = init
            for o in range(0, strips, DEPTH):
                carry = turn(o, carry)
            return carry

        def planes_of(field):
            return [field.at[i] for i in range(planes)]

        for step in range(FINE):
            last = step == FINE - 1
            x = x_in if step == 0 else planes_of(x_next)

            def first_pass(o, g00):
                for i, h, v, six, upper, lower in stencil(x, o):
                    slope = perm[i][h, pl.ds(o, DEPTH)] * (upper - lower) - 6.0 * DIFF
                    value = DIFF * six + slope * v
                    r[i, h, pl.ds(o + 1, DEPTH)] = value
                    g00 = g00 + folded(value * value)
                return g00

            g00 = sweep(first_pass, zero)
            wrap(r)

            def second_pass(o, carry):
                g01, g11 = carry
                for i, h, v, six, _, _ in stencil(planes_of(r), o):
                    value = six * (1.0 / 6.0)
                    p1[i, h, pl.ds(o + 1, DEPTH)] = value
                    g01 = g01 + folded(value * v)
                    g11 = g11 + folded(value * value)
                return g01, g11

            g01, g11 = sweep(second_pass, (zero, zero))
            wrap(p1)

            def third_pass(o, carry):
                g12, g22 = carry
                for i, h, v, six, _, _ in stencil(planes_of(p1), o):
                    value = six * (1.0 / 3.0) - r[i, h, pl.ds(o + 1, DEPTH)]
                    p2[i, h, pl.ds(o + 1, DEPTH)] = value
                    g12 = g12 + folded(value * v)
                    g22 = g22 + folded(value * value)
                return g12, g22

            g12, g22 = sweep(third_pass, (zero, zero))
            wrap(p2)

            def fourth_pass(o, h22):
                rows = []
                for i in range(planes):
                    blocks = [p2[i, h, pl.ds(o + 1, DEPTH + 1)] for h in range(halves)]
                    inner = [b[:DEPTH] for b in blocks]
                    rows.append(inner)
                    upper = uppers(inner)
                    for h in range(halves):
                        h22 = h22 + folded(inner[h] * (blocks[h][1:] + upper[h]))
                for h in range(halves):
                    if planes == 4:
                        h22 = h22 + folded((rows[0][h] + rows[2][h]) * (rows[1][h] + rows[3][h]))
                    else:
                        for i in range(planes):
                            h22 = h22 + folded(rows[i][h] * rows[(i + 1) % planes][h])
                return h22

            h22 = sweep(fourth_pass, zero)
            weights = gram_steps(
                total(g00), total(g01), total(g11), total(g12), total(g22),
                total(h22) * (1.0 / 3.0))
            c0, c1, c2 = (jnp.broadcast_to(c, (DEPTH, SUB, LANES)) for c in weights)

            def last_pass(o, carry):
                for i, h in cells:
                    at = pl.ds(o + 1, DEPTH)
                    value = (x[i][h, at] + c0 * r[i, h, at]) + (c1 * p1[i, h, at] + c2 * p2[i, h, at])
                    if last:
                        outs[i][h, pl.ds(o, DEPTH)] = value
                    else:
                        x_next[i, h, at] = value
                return carry

            sweep(last_pass, 0)
            if not last:
                wrap(x_next)

    return kernel


def fine_steps(active, state_strips, perm_strips, order):
    planes = len(order)
    shape = perm_strips[0].shape
    field = pltpu.VMEM((planes,) + state_strips[0].shape, jnp.float32)
    return pl.pallas_call(
        fine_kernel(order, *shape[:2]),
        out_shape=[jax.ShapeDtypeStruct(shape, jnp.float32)] * planes,
        in_specs=in_smem(1) + in_vmem(2 * planes),
        out_specs=in_vmem(planes),
        scratch_shapes=[field] * 4,
        compiler_params=small_vmem(),
        name="fine_steps",
    )(active, *[state_strips[k] for k in order], *[perm_strips[k] for k in order])


def chosen(which, candidates, h, o):
    value = candidates[0][h, o]
    for k in range(1, len(candidates)):
        value = jnp.where(which == k, candidates[k][h, o], value)
    return value


def coarse_change(which, candidates, own):
    count = len(candidates)
    halves, strips = candidates[0].shape[:2]

    def kernel(choice, *refs):
        ends, own_ref, out = refs[:count], refs[count], refs[count + 1]
        read = lambda h, o: chosen(choice[0], ends, h, o)
        for c, tile in enumerate(restrict_strips(read, halves, strips)):
            out[c] = tile - own_ref[c]

    return pl.pallas_call(
        kernel,
        out_shape=jax.ShapeDtypeStruct(own.shape, jnp.float32),
        in_specs=in_smem(1) + in_vmem(count + 1),
        out_specs=in_vmem(1)[0],
        compiler_params=small_vmem(),
        name="coarse_change",
    )(which, *candidates, own)


def corrected(choice, candidates, ratio, changes, start):
    ny, nz = start.shape
    count, turns = len(candidates), len(changes)
    halves_count, strips = nz // LANES, ny // SUB

    def kernel(which, *refs):
        ends, share = refs[:count], refs[count]
        others = refs[count + 1:count + 1 + turns]
        begin, out, halves, sems = refs[count + 1 + turns:]

        @pl.when(which[1] == 0)
        def _():
            copies = halves_of(begin, halves, sems)
            for copy in copies:
                copy.start()
            leaving = []
            for h, copy in enumerate(copies):
                copy.wait()
                leaving.append(pltpu.make_async_copy(
                    halves.at[h], out.at[:, pl.ds(h * LANES, LANES)], sems.at[h]))
                leaving[h].start()
            for copy in leaving:
                copy.wait()

        @pl.when(which[1] != 0)
        def _():
            copies = []
            for c in range(halves_count // 2):
                drift = jnp.zeros((ny // 2, LANES), jnp.float32)
                for k in reversed(range(turns)):
                    drift = share[c] * (drift + others[k][c])
                for h in (2 * c, 2 * c + 1):
                    wide = exact_dot(drift, pairs(c, h, True))
                    for o in range(strips):
                        first = (o // 2) * SUB
                        value = chosen(which[0], ends, h, o) + wide[first:first + SUB]
                        halves[h, pl.ds(o, SUB, stride=strips)] = value
                    copy = pltpu.make_async_copy(
                        halves.at[h], out.at[:, pl.ds(h * LANES, LANES)], sems.at[h])
                    copy.start()
                    copies.append(copy)
            for copy in copies:
                copy.wait()

    return pl.pallas_call(
        kernel,
        out_shape=jax.ShapeDtypeStruct((ny, nz), jnp.float32),
        in_specs=in_smem(1) + in_vmem(count + 1 + turns) + in_hbm(1),
        out_specs=in_hbm(1)[0],
        scratch_shapes=[pltpu.VMEM((halves_count, ny, LANES), jnp.float32),
                        pltpu.SemaphoreType.DMA((halves_count,))],
        compiler_params=small_vmem(),
        name="corrected",
    )(choice, *candidates, ratio, *changes, pltpu.with_memory_space_constraint(start, pltpu.HBM))


def gathered_body(state, classes, perm_table, rate_table):
    start = state[0, 0]
    kinds = classes[0]
    width, slices = lax.axis_size("space"), lax.axis_size("tm")
    axes = ("space", "tm")
    place = lambda s, t: (s % width) * slices + t
    site = lambda j: (width // 2 - 1 + j % 2) % width
    used = range(slices - 1)

    def to_sites(array, k):
        return lax.ppermute(array, axes, [
            (place(site(j) + k, j), place(site(j), j)) for j in used])

    def from_sites(array, k):
        return lax.ppermute(array, axes, [
            (place(site(j), j), place(site(j) + k, j + 1)) for j in used])

    order = sorted(range(1, width), key=lambda k: (min(k, width - k), -k)) + [0]
    state_planes = {k: to_sites(start, k) for k in order[:-1]}
    state_planes[0] = start
    perm = strips_of_perm(kinds, perm_table)
    perm_strips = {k: to_sites(perm, k) for k in order[:-1]}
    perm_strips[0] = perm
    own, ratio = coarse_parts(start, kinds, rate_table)
    state_strips = dict(zip(order, strips_of_state([state_planes[k] for k in order])))
    turn, plane = lax.axis_index("tm"), lax.axis_index("space")
    here = (turn < slices - 1) & (plane == site(turn))
    ends = fine_steps(here.astype(jnp.int32)[None], state_strips, perm_strips, order)
    candidates = [from_sites(ends[k], k) for k in range(width)]
    which = (plane - site(turn - 1)) % width
    choice = jnp.stack([which, turn]).astype(jnp.int32)
    change = coarse_change(choice, candidates, own)
    changes = [
        lax.ppermute(change, "tm", [(i, i + k) for i in range(1, slices - k)])
        for k in range(1, slices - 1)
    ]
    return corrected(choice, candidates, ratio, changes, start)[None, None]


def body(state, classes, perm_table, rate_table):
    width = lax.axis_size("space")
    one_plane = state.shape[:2] == (1, 1) and classes.shape[0] == 1
    ny, nz = state.shape[2:]
    tiles = ny % (2 * DEPTH * SUB) == 0 and nz % (2 * LANES) == 0
    if one_plane and tiles and 2 < width <= MOST_PLANES and lax.axis_size("tm") > 2:
        return gathered_body(state, classes, perm_table, rate_table)
    return spread_body(state, classes, perm_table, rate_table)


def solution(mesh):
    placed = (
        P(("groups", "tm"), "space", None, None),
        P(("groups", "space"), None, None),
        P(),
        P(),
    )
    return jax.shard_map(
        body,
        mesh=mesh,
        in_specs=placed,
        out_specs=P(("groups", "tm"), "space", None, None),
        check_vma=False,
    )
```

```python
import jax
import jax.numpy as jnp
from jax import lax
from jax.experimental import pallas as pl
from jax.experimental.pallas import tpu as pltpu
from jax.sharding import PartitionSpec as P

ITERS = 3
FINE = 2


DIFF = 2.0
ADV = 0.25

SUB = 8
LANES = 128
DEPTH = 2
MOST_PLANES = 8
VMEM_BYTES = 16 * 1024 * 1024


def with_halo(array, sides, width):
    for axis, dim in sides:
        devices, length = (lax.axis_size(axis), array.shape[dim])
        up = [(i, (i + 1) % devices) for i in range(devices)]
        down = [(j, i) for i, j in up]
        last = lax.slice_in_dim(array, length - width, length, axis=dim)
        first = lax.slice_in_dim(array, 0, width, axis=dim)
        before = lax.ppermute(last, axis, up)
        after = lax.ppermute(first, axis, down)
        array = jnp.concatenate([before, array, after], axis=dim)
    return array


def passed_along(array, axis, by):
    devices = lax.axis_size(axis)
    pairs = [(i, i + by) for i in range(devices) if 0 <= i + by < devices]
    return lax.ppermute(array, axis, pairs)


def lookup(table, classes):
    values = jnp.zeros(classes.shape, jnp.float32)
    for entry in range(table.shape[0]):
        values = jnp.where(classes == entry, table[entry], values)
    return values


def restrict(field):
    cx, ny, nz = field.shape
    return field.reshape(cx, ny // 2, 2, nz // 2, 2).mean(axis=(2, 4))


def prolong(coarse):
    return jnp.repeat(jnp.repeat(coarse, 2, axis=1), 2, axis=2)


def vertical(field):
    zero_plane = jnp.zeros(field.shape[:2] + (1,), jnp.float32)
    upper = jnp.concatenate([field[:, :, 1:], zero_plane], axis=2)
    lower = jnp.concatenate([zero_plane, field[:, :, :-1]], axis=2)
    return (upper, lower)


def operate(field):
    padded = with_halo(field, (("space", 0),), 1)
    upper, lower = vertical(field)
    beside = padded[2:] + padded[:-2]
    beside = beside + jnp.roll(field, -1, 1) + jnp.roll(field, 1, 1)
    beside = beside + upper + lower
    return (1.0 + 6.0 * DIFF) * field - DIFF * beside


def squares(residual):
    return lax.psum(jnp.sum(residual * residual), "space")


def fine_step(field, perm):
    upper, lower = vertical(field)
    rhs = field - ADV * perm * field * (upper - lower)
    solution = field
    residual = rhs - operate(solution)
    direction = residual
    norm_now = squares(residual)
    for step in range(ITERS):
        image = operate(direction)
        alpha = norm_now / lax.psum(jnp.sum(direction * image), "space")
        solution = solution + alpha * direction
        residual = residual - alpha * image
        norm_next = squares(residual)
        direction = residual + norm_next / norm_now * direction
        norm_now = norm_next
    return solution


def spread_body(state, classes, perm_table, rate_table):
    start = state[0]
    perm = lookup(perm_table, classes)
    coarse_ratio = 1.0 / (1.0 + restrict(lookup(rate_table, classes)))
    field = start
    for step in range(FINE):
        field = fine_step(field, perm)
    coarse_start = restrict(start)
    jump = field - prolong(coarse_ratio * coarse_start)
    jump_coarse = restrict(jump)
    first = lax.axis_index("tm") == 0
    factor = jnp.where(first, 0.0, coarse_ratio)
    offset = jnp.where(first, coarse_ratio * coarse_start + jump_coarse, jump_coarse)
    before = passed_along(jump, "tm", 1)
    before_coarse = restrict(before)

    def relay_turn(turn, carry):
        outgoing, received = carry
        received = passed_along(outgoing, "tm", 1)
        return (factor * received + offset, received)

    outgoing, received = lax.fori_loop(
        0, lax.axis_size("tm") - 1, relay_turn, (offset, jnp.zeros_like(offset))
    )
    updated = jnp.where(first, start, before + prolong(received - before_coarse))
    return updated[None]


def in_vmem(count):
    return [pl.BlockSpec(memory_space=pltpu.VMEM)] * count


def anywhere(count):
    return [pl.BlockSpec(memory_space=pl.ANY)] * count


def in_hbm(count):
    return [pl.BlockSpec(memory_space=pltpu.HBM)] * count


def in_smem(count):
    return [pl.BlockSpec(memory_space=pltpu.SMEM)] * count


def small_vmem():
    return pltpu.CompilerParams(vmem_limit_bytes=VMEM_BYTES)


def strips_shape(ny, nz, extra=0):
    return (nz // LANES, ny // SUB + extra, SUB, LANES)


def halves_of(plane, halves, sems):
    return [
        pltpu.make_async_copy(plane.at[:, pl.ds(h * LANES, LANES)], halves.at[h], sems.at[h])
        for h in range(halves.shape[0])
    ]


def strip(halves, h, o, strips):
    return halves[h, pl.ds(o, SUB, stride=strips)]


def pairs(coarse_lane, h, transposed):
    shape = (LANES, LANES)
    fine = lax.broadcasted_iota(jnp.int32, shape, 1 if transposed else 0) + h * LANES
    coarse = lax.broadcasted_iota(jnp.int32, shape, 0 if transposed else 1) + coarse_lane * LANES
    return jnp.where(fine // 2 == coarse, 1.0, 0.0).astype(jnp.bfloat16)


def exact_dot(a, ones):
    total = jnp.zeros((a.shape[0], ones.shape[1]), jnp.float32)
    parts = []
    for _ in range(3):
        part = a.astype(jnp.bfloat16)
        parts.append(part)
        a = a - part.astype(jnp.float32)
    for part in reversed(parts):
        total = total + jnp.dot(part, ones, preferred_element_type=jnp.float32)
    return total


def restrict_strips(read, halves, strips):
    rows = [
        jnp.concatenate([read(h, o) + read(h, o + 1) for o in range(0, strips, 2)], axis=0)
        for h in range(halves)
    ]
    result = []
    for c in range(halves // 2):
        tile = exact_dot(rows[2 * c], pairs(c, 2 * c, False))
        tile = tile + exact_dot(rows[2 * c + 1], pairs(c, 2 * c + 1, False))
        result.append(0.25 * tile)
    return result


def strips_of_perm(classes, table):
    ny, nz = classes.shape
    shape = strips_shape(ny, nz)

    def kernel(values, kinds, out, halves, sems):
        copies = halves_of(kinds, halves, sems)
        for copy in copies:
            copy.start()
        for h in range(shape[0]):
            copies[h].wait()
            for o in range(shape[1]):
                kind = strip(halves, h, o, shape[1])
                value = jnp.zeros((SUB, LANES), jnp.float32)
                for entry in range(table.shape[0]):
                    value = jnp.where(kind == entry, -ADV * values[entry], value)
                out[h, o] = value

    return pl.pallas_call(
        kernel,
        out_shape=jax.ShapeDtypeStruct(shape, jnp.float32),
        in_specs=in_smem(1) + in_hbm(1),
        out_specs=in_vmem(1)[0],
        scratch_shapes=[pltpu.VMEM((shape[0], ny, LANES), jnp.int32),
                        pltpu.SemaphoreType.DMA((shape[0],))],
        compiler_params=small_vmem(),
        name="strips_of_perm",
    )(table, classes)


def strips_of_state(planes):
    count = len(planes)
    ny, nz = planes[0].shape
    halves_count, strips = nz // LANES, ny // SUB

    def kernel(*refs):
        outs, halves, sems = refs[count:2 * count], refs[2 * count], refs[2 * count + 1]
        copies = [halves_of(refs[i], halves.at[i], sems.at[i]) for i in range(count)]
        for row in copies:
            for copy in row:
                copy.start()
        for i in range(count):
            for h in range(halves_count):
                copies[i][h].wait()
                for o in range(strips):
                    value = strip(halves.at[i], h, o, strips)
                    outs[i][h, o + 1] = value
                    if o == 0:
                        outs[i][h, strips + 1] = pltpu.roll(value, SUB - 1, 0)
                    if o == strips - 1:
                        outs[i][h, 0] = pltpu.roll(value, 1, 0)

    return pl.pallas_call(
        kernel,
        out_shape=[jax.ShapeDtypeStruct(strips_shape(ny, nz, 2), jnp.float32)] * count,
        in_specs=anywhere(count),
        out_specs=in_vmem(count),
        scratch_shapes=[pltpu.VMEM((count, halves_count, ny, LANES), jnp.float32),
                        pltpu.SemaphoreType.DMA((count, halves_count))],
        compiler_params=small_vmem(),
        name="strips_of_state",
    )(*planes)


def coarse_parts(state, classes, rate_table):
    ny, nz = state.shape
    halves_count, strips = nz // LANES, ny // SUB
    coarse = (nz // (2 * LANES), ny // 2, LANES)

    def kernel(rates, field, kinds, own, ratio, fields_in, kinds_in, sems):
        copies = halves_of(field, fields_in, sems.at[0]) + halves_of(kinds, kinds_in, sems.at[1])
        for copy in copies:
            copy.start()
        for copy in copies:
            copy.wait()

        def rate(h, o):
            kind = strip(kinds_in, h, o, strips)
            value = jnp.zeros((SUB, LANES), jnp.float32)
            for entry in range(rate_table.shape[0]):
                value = jnp.where(kind == entry, rates[entry], value)
            return value

        for c, tile in enumerate(restrict_strips(rate, halves_count, strips)):
            ratio[c] = 1.0 / (1.0 + tile)
        read = lambda h, o: strip(fields_in, h, o, strips)
        for c, tile in enumerate(restrict_strips(read, halves_count, strips)):
            own[c] = tile

    return pl.pallas_call(
        kernel,
        out_shape=[jax.ShapeDtypeStruct(coarse, jnp.float32)] * 2,
        in_specs=in_smem(1) + in_hbm(2),
        out_specs=in_vmem(2),
        scratch_shapes=[pltpu.VMEM((halves_count, ny, LANES), jnp.float32),
                        pltpu.VMEM((halves_count, ny, LANES), jnp.int32),
                        pltpu.SemaphoreType.DMA((2, halves_count))],
        compiler_params=small_vmem(),
        name="coarse_parts",
    )(rate_table, pltpu.with_memory_space_constraint(state, pltpu.HBM), pltpu.with_memory_space_constraint(classes, pltpu.HBM))


def gram_steps(g00, g01, g11, g12, g22, h22):
    a = 1.0 + 6.0 * DIFF
    b = 6.0 * DIFF
    g02 = 2.0 * g11 - g00
    h00, h01, h02 = g01, g11, g12
    h11, h12 = 0.5 * (g12 + g01), 0.5 * (g22 + g02)
    rr = g00
    alpha0 = rr / (a * g00 - b * h00)
    p, q = 1.0 - a * alpha0, b * alpha0
    new = p * p * g00 + 2.0 * p * q * g01 + q * q * g11
    beta = new / rr
    rr = new
    e, f = p + beta, q
    dd = e * e * g00 + 2.0 * e * f * g01 + f * f * g11
    dmd = e * e * h00 + 2.0 * e * f * h01 + f * f * h11
    alpha1 = rr / (a * dd - b * dmd)
    u = p - alpha1 * (a * e - 0.5 * b * f)
    v = q - alpha1 * (a * f - b * e)
    w = alpha1 * (0.5 * b) * f
    new = (u * u * g00 + v * v * g11 + w * w * g22
           + 2.0 * (u * v * g01 + u * w * g02 + v * w * g12))
    beta = new / rr
    rr = new
    u, v = u + beta * e, v + beta * f
    dd = (u * u * g00 + v * v * g11 + w * w * g22
          + 2.0 * (u * v * g01 + u * w * g02 + v * w * g12))
    dmd = (u * u * h00 + v * v * h11 + w * w * h22
           + 2.0 * (u * v * h01 + u * w * h02 + v * w * h12))
    alpha2 = rr / (a * dd - b * dmd)
    return (alpha0 + alpha1 * e + alpha2 * u, alpha1 * f + alpha2 * v, alpha2 * w)


def fine_kernel(order, halves, strips):
    planes = len(order)

    def kernel(active, *refs):
        @pl.when(active[0] == 1)
        def _():
            steps(*refs)

    def steps(*refs):
        x_in = [refs[order.index(k)] for k in range(planes)]
        perm = [refs[planes + order.index(k)] for k in range(planes)]
        outs = refs[2 * planes:3 * planes]
        x_next, r, p1, p2 = refs[3 * planes:]
        lane = lax.broadcasted_iota(jnp.int32, (DEPTH, SUB, LANES), 2)
        first_lane, last_lane = lane == 0, lane == LANES - 1
        zero = jnp.zeros((SUB, LANES), jnp.float32)
        cells = [(i, h) for i in range(planes) for h in range(halves)]

        def wrap(field):
            for i, h in cells:
                field[i, h, 0] = pltpu.roll(field[i, h, strips], 1, 0)
                field[i, h, strips + 1] = pltpu.roll(field[i, h, 1], SUB - 1, 0)

        def folded(value):
            return jnp.sum(value, axis=0)

        def total(acc):
            return jnp.sum(jnp.sum(acc, axis=1, keepdims=True), axis=0, keepdims=True)

        def uppers(row):
            turned = [pltpu.roll(c, LANES - 1, 2) for c in row]
            ends = turned[1:] + [jnp.zeros_like(row[0])]
            return [jnp.where(last_lane, e, t) for t, e in zip(turned, ends)]

        def lowers(row):
            turned = [pltpu.roll(c, 1, 2) for c in row]
            ends = [jnp.zeros_like(row[0])] + turned[:-1]
            return [jnp.where(first_lane, e, t) for t, e in zip(turned, ends)]

        def beside_planes(column):
            if planes == 4:
                even, odd = column[0] + column[2], column[1] + column[3]
                return [odd, even, odd, even]
            return [column[i - 1] + column[(i + 1) % planes] for i in range(planes)]

        def stencil(field, o):
            blocks = [[field[i][h, pl.ds(o, DEPTH + 2)] for h in range(halves)]
                      for i in range(planes)]
            inner = [[b[1:DEPTH + 1] for b in row] for row in blocks]
            along_x = [beside_planes([inner[i][h] for i in range(planes)]) for h in range(halves)]
            for i in range(planes):
                upper, lower = uppers(inner[i]), lowers(inner[i])
                for h in range(halves):
                    b = blocks[i][h]
                    six = (along_x[h][i] + (b[2:] + b[:DEPTH])) + (upper[h] + lower[h])
                    yield i, h, inner[i][h], six, upper[h], lower[h]

        def sweep(turn, init):
            carry = init
            for o in range(0, strips, DEPTH):
                carry = turn(o, carry)
            return carry

        def planes_of(field):
            return [field.at[i] for i in range(planes)]

        for step in range(FINE):
            last = step == FINE - 1
            x = x_in if step == 0 else planes_of(x_next)

            def first_pass(o, g00):
                for i, h, v, six, upper, lower in stencil(x, o):
                    slope = perm[i][h, pl.ds(o, DEPTH)] * (upper - lower) - 6.0 * DIFF
                    value = DIFF * six + slope * v
                    r[i, h, pl.ds(o + 1, DEPTH)] = value
                    g00 = g00 + folded(value * value)
                return g00

            g00 = sweep(first_pass, zero)
            wrap(r)

            def second_pass(o, carry):
                g01, g11 = carry
                for i, h, v, six, _, _ in stencil(planes_of(r), o):
                    value = six * (1.0 / 6.0)
                    p1[i, h, pl.ds(o + 1, DEPTH)] = value
                    g01 = g01 + folded(value * v)
                    g11 = g11 + folded(value * value)
                return g01, g11

            g01, g11 = sweep(second_pass, (zero, zero))
            wrap(p1)

            def third_pass(o, carry):
                g12, g22 = carry
                for i, h, v, six, _, _ in stencil(planes_of(p1), o):
                    value = six * (1.0 / 3.0) - r[i, h, pl.ds(o + 1, DEPTH)]
                    p2[i, h, pl.ds(o + 1, DEPTH)] = value
                    g12 = g12 + folded(value * v)
                    g22 = g22 + folded(value * value)
                return g12, g22

            g12, g22 = sweep(third_pass, (zero, zero))
            wrap(p2)

            def fourth_pass(o, h22):
                rows = []
                for i in range(planes):
                    blocks = [p2[i, h, pl.ds(o + 1, DEPTH + 1)] for h in range(halves)]
                    inner = [b[:DEPTH] for b in blocks]
                    rows.append(inner)
                    upper = uppers(inner)
                    for h in range(halves):
                        h22 = h22 + folded(inner[h] * (blocks[h][1:] + upper[h]))
                for h in range(halves):
                    if planes == 4:
                        h22 = h22 + folded((rows[0][h] + rows[2][h]) * (rows[1][h] + rows[3][h]))
                    else:
                        for i in range(planes):
                            h22 = h22 + folded(rows[i][h] * rows[(i + 1) % planes][h])
                return h22

            h22 = sweep(fourth_pass, zero)
            weights = gram_steps(
                total(g00), total(g01), total(g11), total(g12), total(g22),
                total(h22) * (1.0 / 3.0))
            c0, c1, c2 = (jnp.broadcast_to(c, (DEPTH, SUB, LANES)) for c in weights)

            def last_pass(o, carry):
                for i, h in cells:
                    at = pl.ds(o + 1, DEPTH)
                    value = (x[i][h, at] + c0 * r[i, h, at]) + (c1 * p1[i, h, at] + c2 * p2[i, h, at])
                    if last:
                        outs[i][h, pl.ds(o, DEPTH)] = value
                    else:
                        x_next[i, h, at] = value
                return carry

            sweep(last_pass, 0)
            if not last:
                wrap(x_next)

    return kernel


def fine_steps(active, state_strips, perm_strips, order):
    planes = len(order)
    shape = perm_strips[0].shape
    field = pltpu.VMEM((planes,) + state_strips[0].shape, jnp.float32)
    return pl.pallas_call(
        fine_kernel(order, *shape[:2]),
        out_shape=[jax.ShapeDtypeStruct(shape, jnp.float32)] * planes,
        in_specs=in_smem(1) + in_vmem(2 * planes),
        out_specs=in_vmem(planes),
        scratch_shapes=[field] * 4,
        compiler_params=small_vmem(),
        name="fine_steps",
    )(active, *[state_strips[k] for k in order], *[perm_strips[k] for k in order])


def chosen(which, candidates, h, o):
    value = candidates[0][h, o]
    for k in range(1, len(candidates)):
        value = jnp.where(which == k, candidates[k][h, o], value)
    return value


def coarse_change(which, candidates, own):
    count = len(candidates)
    halves, strips = candidates[0].shape[:2]

    def kernel(choice, *refs):
        ends, own_ref, out = refs[:count], refs[count], refs[count + 1]
        for k in range(count):
            @pl.when(choice[0] == k)
            def _():
                read = lambda h, o: ends[k][h, o]
                for c, tile in enumerate(restrict_strips(read, halves, strips)):
                    out[c] = tile - own_ref[c]

    return pl.pallas_call(
        kernel,
        out_shape=jax.ShapeDtypeStruct(own.shape, jnp.float32),
        in_specs=in_smem(1) + in_vmem(count + 1),
        out_specs=in_vmem(1)[0],
        compiler_params=small_vmem(),
        name="coarse_change",
    )(which, *candidates, own)


def corrected(choice, candidates, ratio, changes, start):
    ny, nz = start.shape
    count, turns = len(candidates), len(changes)
    halves_count, strips = nz // LANES, ny // SUB

    def kernel(which, *refs):
        ends, share = refs[:count], refs[count]
        others = refs[count + 1:count + 1 + turns]
        begin, out, halves, sems = refs[count + 1 + turns:]

        @pl.when(which[1] == 0)
        def _():
            copies = halves_of(begin, halves, sems)
            for copy in copies:
                copy.start()
            leaving = []
            for h, copy in enumerate(copies):
                copy.wait()
                leaving.append(pltpu.make_async_copy(
                    halves.at[h], out.at[:, pl.ds(h * LANES, LANES)], sems.at[h]))
                leaving[h].start()
            for copy in leaving:
                copy.wait()

        @pl.when(which[1] != 0)
        def _():
            copies = []
            for c in range(halves_count // 2):
                drift = jnp.zeros((ny // 2, LANES), jnp.float32)
                for k in reversed(range(turns)):
                    drift = share[c] * (drift + others[k][c])
                for h in (2 * c, 2 * c + 1):
                    wide = exact_dot(drift, pairs(c, h, True))
                    for o in range(strips):
                        first = (o // 2) * SUB
                        value = chosen(which[0], ends, h, o) + wide[first:first + SUB]
                        halves[h, pl.ds(o, SUB, stride=strips)] = value
                    copy = pltpu.make_async_copy(
                        halves.at[h], out.at[:, pl.ds(h * LANES, LANES)], sems.at[h])
                    copy.start()
                    copies.append(copy)
            for copy in copies:
                copy.wait()

    return pl.pallas_call(
        kernel,
        out_shape=jax.ShapeDtypeStruct((ny, nz), jnp.float32),
        in_specs=in_smem(1) + in_vmem(count + 1 + turns) + in_hbm(1),
        out_specs=in_hbm(1)[0],
        scratch_shapes=[pltpu.VMEM((halves_count, ny, LANES), jnp.float32),
                        pltpu.SemaphoreType.DMA((halves_count,))],
        compiler_params=small_vmem(),
        name="corrected",
    )(choice, *candidates, ratio, *changes, pltpu.with_memory_space_constraint(start, pltpu.HBM))


def gathered_body(state, classes, perm_table, rate_table):
    start = state[0, 0]
    kinds = classes[0]
    width, slices = lax.axis_size("space"), lax.axis_size("tm")
    axes = ("space", "tm")
    place = lambda s, t: (s % width) * slices + t
    site = lambda j: (width // 2 - 1 + j % 2) % width
    used = range(slices - 1)

    def to_sites(array, k):
        return lax.ppermute(array, axes, [
            (place(site(j) + k, j), place(site(j), j)) for j in used])

    def from_sites(array, k):
        return lax.ppermute(array, axes, [
            (place(site(j), j), place(site(j) + k, j + 1)) for j in used])

    order = sorted(range(1, width), key=lambda k: (min(k, width - k), -k)) + [0]
    state_planes = {k: to_sites(start, k) for k in order[:-1]}
    state_planes[0] = start
    perm = strips_of_perm(kinds, perm_table)
    perm_strips = {k: to_sites(perm, k) for k in order[:-1]}
    perm_strips[0] = perm
    own, ratio = coarse_parts(start, kinds, rate_table)
    state_strips = dict(zip(order, strips_of_state([state_planes[k] for k in order])))
    turn, plane = lax.axis_index("tm"), lax.axis_index("space")
    here = (turn < slices - 1) & (plane == site(turn))
    ends = fine_steps(here.astype(jnp.int32)[None], state_strips, perm_strips, order)
    candidates = [from_sites(ends[k], k) for k in range(width)]
    which = (plane - site(turn - 1)) % width
    choice = jnp.stack([which, turn]).astype(jnp.int32)
    change = coarse_change(choice, candidates, own)
    changes = [
        lax.ppermute(change, "tm", [(i, i + k) for i in range(1, slices - k)])
        for k in range(1, slices - 1)
    ]
    return corrected(choice, candidates, ratio, changes, start)[None, None]


def body(state, classes, perm_table, rate_table):
    width = lax.axis_size("space")
    one_plane = state.shape[:2] == (1, 1) and classes.shape[0] == 1
    ny, nz = state.shape[2:]
    tiles = ny % (2 * DEPTH * SUB) == 0 and nz % (2 * LANES) == 0
    if one_plane and tiles and 2 < width <= MOST_PLANES and lax.axis_size("tm") > 2:
        return gathered_body(state, classes, perm_table, rate_table)
    return spread_body(state, classes, perm_table, rate_table)


def solution(mesh):
    placed = (
        P(("groups", "tm"), "space", None, None),
        P(("groups", "space"), None, None),
        P(),
        P(),
    )
    return jax.shard_map(
        body,
        mesh=mesh,
        in_specs=placed,
        out_specs=P(("groups", "tm"), "space", None, None),
        check_vma=False,
    )
```
